256 devices in a mesh: gx: 32 (over x, z), gy: 8 (over y, core).
Axes of the slice: x: 4, y: 4, z: 8, core: 2. Of those that a mesh axis runs over, the one named last changes fastest.
Arguments:
- point_counts: int32 [512, 128, 128], P('gx', 'gy'), may hold values from 0 to 16
- face_counts: int32 [3, 512, 128, 128], P(None, 'gx', 'gy'), may hold values from -12 to 12, as said below
Outputs:
- solution: float32 [512, 128, 128], P('gx', 'gy')
- residual: float32 [512, 128, 128], P('gx', 'gy')
The draws below stay inside these ranges and needn't reach their ends.
Inputs may be any that keep to these rules, and one draw needn't show every extreme that they name: `face_counts`: signed count of oriented points splatted onto each upper face.
All inputs are finite; a program needn't handle non-finite values.
Results may differ from the reference program's by a relative error of at most 0.0003.
Values may be sent and summed in bfloat16 or wider, within the bound.
A program may use at most 64 MiB of HBM per device.

```python
import jax
import jax.numpy as jnp

NZ = 128
LEVELS = 3
CYCLES = 2
PRE = 2
POST = 2
COARSE_ITERS = 6
NX = 512
NY = 128


def draw_point_counts(key, part):
    pos_x = jnp.arange(NX, dtype=jnp.int32)[:, None, None]
    pos_y = jnp.arange(NY, dtype=jnp.int32)[None, :, None]
    pos_z = jnp.arange(NZ, dtype=jnp.int32)[None, None, :]
    spread_sq = (NX // 2) ** 2 + (NY // 2) ** 2
    height = NZ // 4 + NZ // 2 * ((pos_x - NX // 2) ** 2 + (pos_y - NY // 2) ** 2) // spread_sq
    inside = jnp.abs(pos_z - height) <= 1
    key_band, key_noise = jax.random.split(key)
    band_counts = jax.random.randint(key_band, (NX, NY, NZ), 1, 17, dtype=jnp.int32)
    stray_points = (jax.random.randint(key_noise, (NX, NY, NZ), 0, 64, dtype=jnp.int32) == 0).astype(jnp.int32)
    counts = jnp.where(inside, band_counts, stray_points)
    return counts.at[0, 0, 3 * NZ // 4].set(16)


def draw_face_counts(key, part):
    pos_x = jnp.arange(NX, dtype=jnp.int32)[None, :, None, None]
    pos_y = jnp.arange(NY, dtype=jnp.int32)[None, None, :, None]
    amplitude = 2 + 6 * pos_x // NX + 6 * pos_y // NY
    amplitude = jnp.broadcast_to(amplitude, (3, NX, NY, NZ))
    values = jax.random.randint(key, (3, NX, NY, NZ), -amplitude, amplitude + 1, dtype=jnp.int32)
    values = values.at[0, NX - 1, NY - 1, 0].set(12)
    return values.at[1, NX - 1, NY - 1, 0].set(-12)


def setup_inputs(seed: int = 0) -> dict:
    splits = jax.random.split(jax.random.key(seed), 3)
    return {
        "point_counts": draw_point_counts(jax.random.fold_in(splits[2], 71), 0),
        "face_counts": draw_face_counts(jax.random.fold_in(splits[2], 71), 0),
    }


screen_weight = 0.25
flux_scale = 0.125
low_edge = 0.3
high_edge = 2.0


def neighbour_sum(padded):
    total = padded[2:, 1:-1, 1:-1] + padded[:-2, 1:-1, 1:-1]
    total = total + padded[1:-1, 2:, 1:-1] + padded[1:-1, :-2, 1:-1]
    total = total + padded[1:-1, 1:-1, 2:] + padded[1:-1, 1:-1, :-2]
    return total


def operate(field, screen, factor):
    return (6.0 * field - neighbour_sum(jnp.pad(field, 1))) * factor + screen * field


def restrict(field):
    size_x, size_y, size_z = field.shape
    blocks = field.reshape(size_x // 2, 2, size_y // 2, 2, size_z // 2, 2)
    return blocks.sum(axis=(1, 3, 5)) * 0.125


def prolong(field):
    size_x, size_y, size_z = field.shape
    spread_out = jnp.broadcast_to(field[:, None, :, None, :, None], (size_x, 2, size_y, 2, size_z, 2))
    return spread_out.reshape(2 * size_x, 2 * size_y, 2 * size_z)


def smooth(iterate, target, screen, inv_diag, factor, step_count):
    centre = 0.5 * (high_edge + low_edge)
    radius = 0.5 * (high_edge - low_edge)
    spread_ratio = centre / radius
    momentum = 1.0 / spread_ratio
    correction = (target - operate(iterate, screen, factor)) * inv_diag
    update = correction * (1.0 / centre)
    iterate = iterate + update
    for step in range(1, step_count):
        momentum_next = 1.0 / (2.0 * spread_ratio - momentum)
        correction = (target - operate(iterate, screen, factor)) * inv_diag
        update = (momentum_next * momentum) * update + (2.0 * momentum_next / radius) * correction
        iterate = iterate + update
        momentum = momentum_next
    return iterate


def coarse_solve(target, screen, factor):
    iterate = jnp.zeros_like(target)
    remain = target
    search = target
    norm_now = jnp.sum(remain * remain)
    for step in range(COARSE_ITERS):
        image = operate(search, screen, factor)
        step_length = norm_now / jnp.sum(search * image)
        iterate = iterate + step_length * search
        if step + 1 < COARSE_ITERS:
            remain = remain - step_length * image
            norm_next = jnp.sum(remain * remain)
            search = remain + (norm_next / norm_now) * search
            norm_now = norm_next
    return iterate


def vcycle(iterate, target, level_index, screens, inv_diags, factors):
    iterate = smooth(iterate, target, screens[level_index], inv_diags[level_index], factors[level_index], PRE)
    remain = target - operate(iterate, screens[level_index], factors[level_index])
    coarse_target = restrict(remain)
    if level_index + 1 == LEVELS:
        coarse_error = coarse_solve(coarse_target, screens[LEVELS], factors[LEVELS])
    else:
        coarse_error = vcycle(jnp.zeros_like(coarse_target), coarse_target, level_index + 1, screens, inv_diags, factors)
    iterate = iterate + prolong(coarse_error)
    return smooth(iterate, target, screens[level_index], inv_diags[level_index], factors[level_index], POST)


def reference(point_counts, face_counts):
    fluxes = face_counts.astype(jnp.float32) * flux_scale
    lower_x = jnp.pad(fluxes[0], ((1, 0), (0, 0), (0, 0)))[:-1]
    lower_y = jnp.pad(fluxes[1], ((0, 0), (1, 0), (0, 0)))[:, :-1]
    lower_z = jnp.pad(fluxes[2], ((0, 0), (0, 0), (1, 0)))[:, :, :-1]
    source = (lower_x - fluxes[0]) + (lower_y - fluxes[1]) + (lower_z - fluxes[2])
    screens = [point_counts.astype(jnp.float32) * screen_weight]
    for level_index in range(LEVELS):
        screens.append(restrict(screens[-1]))
    factors = [0.25 ** level_index for level_index in range(LEVELS + 1)]
    inv_diags = [1.0 / (6.0 * factors[level_index] + screens[level_index]) for level_index in range(LEVELS)]
    solution = jnp.zeros_like(source)
    for cycle_index in range(CYCLES):
        solution = vcycle(solution, source, 0, screens, inv_diags, factors)
    residual = source - operate(solution, screens[0], factors[0])
    return solution, residual
```

```python
import functools

import jax
import jax.numpy as jnp
from jax import lax
from jax.experimental import pallas as pl
from jax.experimental.pallas import tpu as pltpu
from jax.sharding import PartitionSpec as P


MESH = pl.DeviceIdType.MESH
F32 = jnp.float32
BF16 = jnp.bfloat16
NEIGH = tuple((dx, dy) for dx in (-1, 0, 1) for dy in (-1, 0, 1) if (dx, dy) != (0, 0))

CENTRE = 0.5 * (2.0 + 0.3)
RADIUS = 0.5 * (2.0 - 0.3)
RATIO = CENTRE / RADIUS
MOM = 1.0 / RATIO
MOM2 = 1.0 / (2.0 * RATIO - MOM)
C1 = 1.0 / CENTRE
CA = MOM2 * MOM
CB = 2.0 * MOM2 / RADIUS
COARSE_ITERS = 6


def lanes(shape):
    return lax.broadcasted_iota(jnp.int32, shape, len(shape) - 1)


def rows(shape):
    return lax.broadcasted_iota(jnp.int32, shape, len(shape) - 2)


def roll(v, shift, axis):
    return pltpu.roll(v, shift, axis)


def zpair(v, width):
    axis = v.ndim - 1
    low = (lanes(v.shape) & width) == 0
    return v + jnp.where(low, roll(v, 128 - width, axis), roll(v, width, axis))


def side_sum(c, up, dn, shift):
    ax = c.ndim - 2
    count = c.shape[ax]
    lane = lanes(c.shape)
    total = up + dn
    total = total + (roll(c, 1, ax) + roll(c, count - 1, ax))
    low = jnp.where(lane < shift, 0.0, roll(c, shift, ax + 1))
    high = jnp.where(lane >= 128 - shift, 0.0, roll(c, 128 - shift, ax + 1))
    return total + (low + high)


def sweep(lo, hi, step, body):
    def one(k, carry):
        body(lo + k * step)
        return carry

    lax.fori_loop(0, (hi - lo) // step, one, 0)


class Level:
    def __init__(self, x, y, d, g, s, inv, depth, step):
        self.x, self.y, self.d, self.g, self.s, self.inv = x, y, d, g, s, inv
        self.shift = 2**depth
        self.factor = 0.25**depth
        self.step = step

    def apply(self, src, i, n):
        c = src[pl.ds(i + 1, n)]
        around = side_sum(c, src[pl.ds(i + 2, n)], src[pl.ds(i, n)], self.shift)
        return c, (6.0 * c - around) * self.factor + self.s[pl.ds(i, n)] * c

    def first_zero(self, lo, hi):
        n = self.step

        def body(i):
            self.x[pl.ds(i + 1, n)] = self.g[pl.ds(i, n)] * self.inv[pl.ds(i, n)] * C1

        sweep(lo, hi, n, body)

    def second_zero(self, lo, hi):
        n = self.step

        def body(i):
            c, image = self.apply(self.x, i, n)
            z = (self.g[pl.ds(i, n)] - image) * self.inv[pl.ds(i, n)]
            self.y[pl.ds(i + 1, n)] = c + (CA * c + CB * z)

        sweep(lo, hi, n, body)

    def pass_one(self, lo, hi):
        n = self.step

        def body(i):
            c, image = self.apply(self.y, i, n)
            d = (self.g[pl.ds(i, n)] - image) * self.inv[pl.ds(i, n)] * C1
            self.d[pl.ds(i, n)] = d
            self.x[pl.ds(i + 1, n)] = c + d

        sweep(lo, hi, n, body)

    def pass_two(self, lo, hi):
        n = self.step

        def body(i):
            c, image = self.apply(self.x, i, n)
            z = (self.g[pl.ds(i, n)] - image) * self.inv[pl.ds(i, n)]
            self.y[pl.ds(i + 1, n)] = c + (CA * self.d[pl.ds(i, n)] + CB * z)

        sweep(lo, hi, n, body)

    def residual(self, lo, hi, store):
        n = self.step

        def body(i):
            _, image = self.apply(self.y, i, n)
            store(i, n, self.g[pl.ds(i, n)] - image)

        sweep(lo, hi, n, body)


def scratch_list(ngx):
    v = pltpu.VMEM
    return (
        ("fcv", v((3, 16, 16, 128), jnp.int32)),
        ("pcv", v((16, 16, 128), jnp.int32)),
        ("ext", v((32, 4, 16, 128), BF16)),
        ("exs", v((2, 16, 128), BF16)),
        ("rex", v((8, 2, 16, 128), BF16)),
        ("s1p", v((4, 16, 128), BF16)),
        ("rs1", v((8, 4, 16, 128), BF16)),
        ("scrown", v((16, 16, 128), F32)),
        ("s1own", v((8, 8, 128), F32)),
        ("fy1", v((32, 128), F32)),
        ("fy2", v((32, 128), F32)),
        ("x0", v((34, 32, 128), F32)),
        ("y0", v((34, 32, 128), F32)),
        ("d0", v((32, 32, 128), F32)),
        ("g0", v((32, 32, 128), F32)),
        ("s0", v((32, 32, 128), F32)),
        ("i0", v((32, 32, 128), F32)),
        ("r0", v((16, 16, 128), F32)),
        ("pe0", v((16, 32, 128), F32)),
        ("pk", v((2, 4, 8, 128), F32)),
        ("rb", v((2, 8, 4, 8, 128), F32)),
        ("x1", v((26, 24, 128), F32)),
        ("y1", v((26, 24, 128), F32)),
        ("d1", v((24, 24, 128), F32)),
        ("g1", v((24, 24, 128), F32)),
        ("s1", v((24, 24, 128), F32)),
        ("i1", v((24, 24, 128), F32)),
        ("r1", v((16, 24, 128), F32)),
        ("pe1", v((16, 24, 128), F32)),
        ("s2t", v((8, 8, 128), F32)),
        ("i2t", v((8, 8, 128), F32)),
        ("rs2", v((8, 8, 8, 128), F32)),
        ("g2t", v((2, 8, 8, 128), F32)),
        ("rg2", v((2, 8, 8, 8, 128), F32)),
        ("x2", v((18, 16, 128), F32)),
        ("y2", v((18, 16, 128), F32)),
        ("d2", v((16, 16, 128), F32)),
        ("g2", v((16, 16, 128), F32)),
        ("s2", v((16, 16, 128), F32)),
        ("i2", v((16, 16, 128), F32)),
        ("pe2", v((8, 16, 128), F32)),
        ("tile", v((3, 8, 128), F32)),
        ("p1", v((3, 7, 8, 128), F32)),
        ("agb", v((3, ngx, 8, 128), F32)),
        ("s3", v((ngx // 2, 8, 128), F32)),
        ("e3", v((ngx // 2, 8, 128), F32)),
        ("snd", pltpu.SemaphoreType.DMA((8, 8))),
        ("rcv", pltpu.SemaphoreType.DMA((8, 8))),
        ("ags", pltpu.SemaphoreType.DMA((3, 4))),
        ("loc", pltpu.SemaphoreType.DMA((2,))),
    )


EX_IN, EX_FACE, EX_S1, EX_S2, EX_B, EX_G = 0, 1, 2, 3, 4, 6


def kernel(ngx, ngy, names, pc_hbm, fc_hbm, sol_ref, res_ref, *scratch):
    m = dict(zip(names, scratch))
    gx = lax.axis_index("gx")
    gy = lax.axis_index("gy")
    half = ngx // 2
    nx0, ny0 = 16 * ngx, 16 * ngy

    def wrap_x(v):
        return lax.rem(v + ngx, ngx)

    def wrap_y(v):
        return lax.rem(v + ngy, ngy)

    copy_p = pltpu.make_async_copy(pc_hbm, m["pcv"], m["loc"].at[0])
    copy_f = pltpu.make_async_copy(fc_hbm, m["fcv"], m["loc"].at[1])
    copy_p.start()
    copy_f.start()

    barrier = pltpu.get_barrier_semaphore()
    peers = 0
    for o in range(1, ngy):
        pl.semaphore_signal(barrier, inc=1, device_id=(gx, wrap_y(gy + o)), device_id_type=MESH)
        peers += 1

    def greet(o, carry):
        pl.semaphore_signal(barrier, inc=1, device_id=(wrap_x(gx + o), gy), device_id_type=MESH)
        return carry

    lax.fori_loop(1, ngx, greet, 0)
    peers += ngx - 1
    for dx, dy in NEIGH:
        if dx != 0 and dy != 0:
            pl.semaphore_signal(
                barrier, inc=1, device_id=(wrap_x(gx + dx), wrap_y(gy + dy)), device_id_type=MESH
            )
            peers += 1

    for name in ("x0", "y0", "x1", "y1", "x2", "y2"):
        ref = m[name]
        last = ref.shape[0] - 1
        ref[0] = jnp.zeros(ref.shape[1:], F32)
        ref[last] = jnp.zeros(ref.shape[1:], F32)

    copy_p.wait()
    copy_f.wait()
    fcv, pcv = m["fcv"], m["pcv"]

    def own_row(i):
        f0 = fcv[0, i].astype(F32) * 0.125
        before = fcv[0, jnp.maximum(i - 1, 0)].astype(F32) * 0.125
        f1 = fcv[1, i].astype(F32) * 0.125
        f2 = fcv[2, i].astype(F32) * 0.125
        low_x = jnp.where(i > 0, before, 0.0)
        low_y = jnp.where(rows(f1.shape) == 0, 0.0, roll(f1, 1, 0))
        low_z = jnp.where(lanes(f2.shape) == 0, 0.0, roll(f2, 1, 1))
        src = (low_x - f0) + (low_y - f1) + (low_z - f2)
        scr = pcv[i].astype(F32) * 0.25
        m["scrown"][i] = scr
        for t in range(2):
            part = slice(8 * t, 8 * t + 8)
            m["ext"][i + 8, t + 1] = jnp.concatenate([src[part], scr[part]], axis=0).astype(BF16)

    sweep(0, 16, 1, own_row)

    tile_shape = (8, 128)
    sub = rows(tile_shape)
    lane = lanes(tile_shape)
    face_x = fcv[0, 15].astype(F32) * 0.125
    own_fx = [face_x[0:8], face_x[8:16]]
    own_fy = []
    for h in range(2):
        total = jnp.zeros(tile_shape, F32)
        for r in range(8):
            row = fcv[1, 8 * h + r, 15:16].astype(F32) * 0.125
            total = jnp.where(sub == r, row, total)
        own_fy.append(total)
    for t in range(2):
        m["exs"][t] = jnp.concatenate([own_fx[t], own_fy[t]], axis=0).astype(BF16)

    own1 = []
    for i in range(8):
        total = jnp.zeros(tile_shape, F32)
        for q in range(2):
            for j in range(2):
                total = total + m["scrown"][2 * i + q, pl.ds(j, 8, stride=2), :]
        v = zpair(total, 1) * 0.125
        m["s1own"][i] = v
        own1.append(v)
    for k in range(4):
        m["s1p"][k] = jnp.concatenate([own1[2 * k], own1[2 * k + 1]], axis=0).astype(BF16)

    def pack3(parts):
        slot = lane & 3
        total = jnp.zeros(tile_shape, F32)
        for xi in range(2):
            for yi in range(2):
                total = jnp.where(slot == 2 * xi + yi, parts[xi][yi], total)
        return total

    own3 = []
    for xi in range(2):
        pair = jnp.zeros((4, 128), F32)
        for q in range(2):
            quad = jnp.zeros((4, 128), F32)
            for h in range(2):
                for j in range(2):
                    quad = quad + m["s1own"][4 * xi + 2 * q + h, pl.ds(j, 4, stride=2), :]
            pair = pair + zpair(quad, 2) * 0.125
        pair = zpair(pair, 4) * 0.125
        own3.append([pair[0:1] + pair[1:2], pair[2:3] + pair[3:4]])
    m["tile"][2] = pack3(own3)

    pl.semaphore_wait(barrier, peers)

    sent = []

    def exchange(kind, make):
        copies = []
        for n, (dx, dy) in enumerate(NEIGH):
            src, dst = make(n, dx, dy)
            copy = pltpu.make_async_remote_copy(
                src_ref=src,
                dst_ref=dst,
                send_sem=m["snd"].at[kind, n],
                recv_sem=m["rcv"].at[kind, n],
                device_id=(wrap_x(gx + dx), wrap_y(gy + dy)),
                device_id_type=MESH,
            )
            copy.start()
            copies.append(copy)
        sent.extend(copies)
        return copies

    def arrive(copies):
        for copy in copies:
            copy.wait_recv()

    def from_source(px, py):
        return NEIGH.index((-px, -py))

    spans = {1: (8, 8, 0), 0: (0, 16, 8), -1: (0, 8, 24)}
    tiles = {1: (1, 1, 0), 0: (0, 2, 1), -1: (0, 1, 3)}

    def make_in(n, dx, dy):
        xs, xn, xd = spans[dx]
        ys, yn, yd = tiles[dy]
        src = m["ext"].at[pl.ds(xs + 8, xn), pl.ds(ys + 1, yn)]
        dst = m["ext"].at[pl.ds(xd, xn), pl.ds(yd, yn)]
        return src, dst

    copies_face = exchange(EX_FACE, lambda n, dx, dy: (m["exs"], m["rex"].at[n]))
    copies_in = exchange(EX_IN, make_in)
    copies_s1 = exchange(EX_S1, lambda n, dx, dy: (m["s1p"], m["rs1"].at[n]))

    def gather_one(c):
        for o in range(1, ngy):
            pltpu.make_async_remote_copy(
                src_ref=m["tile"].at[c],
                dst_ref=m["p1"].at[c, o - 1],
                send_sem=m["ags"].at[c, 0],
                recv_sem=m["ags"].at[c, 1],
                device_id=(gx, wrap_y(gy + o)),
                device_id_type=MESH,
            ).start()

    def wait_bytes(ref, sem):
        pltpu.make_async_copy(ref, ref, sem).wait()

    def gather_two(c):
        wait_bytes(m["p1"].at[c, pl.ds(0, ngy - 1)], m["ags"].at[c, 1])
        total = jnp.where(sub == gy, m["tile"][c], 0.0)
        for o in range(1, ngy):
            total = jnp.where(sub == wrap_y(gy - o), m["p1"][c, o - 1], total)
        m["agb"][c, gx] = total

        def send(o, carry):
            pltpu.make_async_remote_copy(
                src_ref=m["agb"].at[c, gx],
                dst_ref=m["agb"].at[c, gx],
                send_sem=m["ags"].at[c, 2],
                recv_sem=m["ags"].at[c, 3],
                device_id=(wrap_x(gx + o), gy),
                device_id_type=MESH,
            ).start()
            return carry

        lax.fori_loop(1, ngx, send, 0)

    def gather_done(c):
        wait_bytes(m["agb"].at[c, pl.ds(0, ngx - 1)], m["ags"].at[c, 3])
        full = (half, 8, 128)
        return jnp.where((lanes(full) & 4) == 0, m["agb"][c, 0:half], m["agb"][c, half:ngx])

    gather_one(2)

    arrive(copies_face)
    gate_x = jnp.where(gx > 0, 1.0, 0.0)
    gate_y = jnp.where(gy > 0, 1.0, 0.0)

    def face(px, py, t):
        return m["rex"][from_source(px, py), t].astype(F32)

    m["fy1"][0:8] = face(-1, -1, 1)[8:16] * gate_y
    m["fy1"][8:16] = face(0, -1, 0)[8:16] * gate_y
    m["fy1"][16:24] = face(0, -1, 1)[8:16] * gate_y
    m["fy1"][24:32] = face(1, -1, 0)[8:16] * gate_y
    m["fy2"][0:8] = face(-1, 0, 1)[8:16]
    m["fy2"][8:16] = own_fy[0]
    m["fy2"][16:24] = own_fy[1]
    m["fy2"][24:32] = face(1, 0, 0)[8:16]
    arrive(copies_in)

    def inside(shape, i, level, off_x, off_y):
        x = lax.broadcasted_iota(jnp.int32, shape, 0) + (i - off_x + gx * (16 >> level))
        y = rows(shape) + (gy * (16 >> level) - off_y)
        return (x >= 0) & (x < (nx0 >> level)) & (y >= 0) & (y < (ny0 >> level))

    def inverse(scr, i, level, off):
        mask = inside(scr.shape, i, level, off, off)
        return jnp.where(mask, 1.0 / (6.0 * 0.25**level + scr), 0.0)

    def unpack_in(i):
        for t in range(4):
            pair = m["ext"][i, t].astype(F32)
            src = pair[0:8]
            if t == 1:
                src = src + jnp.where(sub == 0, m["fy1"][pl.ds(i, 1)], 0.0)
            if t == 3:
                src = src + jnp.where(sub == 0, m["fy2"][pl.ds(i, 1)], 0.0)
            m["g0"][i, 8 * t : 8 * t + 8] = src
            m["s0"][i, 8 * t : 8 * t + 8] = pair[8:16]

    sweep(0, 32, 1, unpack_in)
    for t, (py, k) in enumerate(((-1, 1), (0, 0), (0, 1), (1, 0))):
        part = slice(8 * t, 8 * t + 8)
        m["g0"][8, part] = m["g0"][8, part] + face(-1, py, k)[0:8] * gate_x
        upper = own_fx[k] if py == 0 else face(0, py, k)[0:8]
        m["g0"][24, part] = m["g0"][24, part] + upper

    lv0 = Level(m["x0"], m["y0"], m["d0"], m["g0"], m["s0"], m["i0"], 0, 4)
    lv1 = Level(m["x1"], m["y1"], m["d1"], m["g1"], m["s1"], m["i1"], 1, 4)
    lv2 = Level(m["x2"], m["y2"], m["d2"], m["g2"], m["s2"], m["i2"], 2, 8)

    def make_inv(level, step, count, off):
        def body(i):
            level.inv[pl.ds(i, step)] = inverse(level.s[pl.ds(i, step)], i, level.shift.bit_length() - 1, off)

        sweep(0, count, step, body)

    make_inv(lv0, 4, 32, 8)

    odd = (lane & 1) == 1
    copies_b = [None, None]
    copies_g = [None, None]

    def send_b(c):
        def store(i, n, r):
            m["r0"][pl.ds(i - 8, n)] = r[:, 8:24]

        lv0.residual(8, 24, store)
        fine = []
        for i in range(8):
            total = jnp.zeros(tile_shape, F32)
            for q in range(2):
                for j in range(2):
                    total = total + m["r0"][2 * i + q, pl.ds(j, 8, stride=2), :]
            v = zpair(total, 1) * 0.125
            m["g1"][8 + i, 8:16] = v
            fine.append(v)
        for k in range(4):
            m["pk"][c, k] = jnp.where(odd, fine[2 * k + 1], fine[2 * k])
        copies_b[c] = exchange(EX_B + c, lambda n, dx, dy: (m["pk"].at[c], m["rb"].at[c, n]))

    def take_b(c):
        arrive(copies_b[c])
        for n, (dx, dy) in enumerate(NEIGH):
            base = 8 - 8 * dx
            part = slice(8 - 8 * dy, 16 - 8 * dy)
            for k in range(4):
                v = m["rb"][c, n, k]
                m["g1"][base + 2 * k, part] = jnp.where(odd, roll(v, 1, 1), v)
                m["g1"][base + 2 * k + 1, part] = jnp.where(odd, v, roll(v, 127, 1))

    def setup_level1():
        arrive(copies_s1)
        for i in range(8):
            m["s1"][8 + i, 8:16] = m["s1own"][i]
        for n, (dx, dy) in enumerate(NEIGH):
            base = 8 - 8 * dx
            part = slice(8 - 8 * dy, 16 - 8 * dy)
            for k in range(4):
                v = m["rs1"][n, k].astype(F32)
                m["s1"][base + 2 * k, part] = v[0:8]
                m["s1"][base + 2 * k + 1, part] = v[8:16]
        make_inv(lv1, 4, 24, 8)
        for i in range(8):
            total = jnp.zeros(tile_shape, F32)
            for q in range(2):
                for j in range(2):
                    total = total + m["s1"][4 + 2 * i + q, pl.ds(4 + j, 8, stride=2), :]
            m["s2t"][i] = zpair(total, 2) * 0.125
        m["i2t"][...] = inverse(m["s2t"][...], 0, 2, 2)

    def exchange_tile(kind, src, dst):
        def make(n, dx, dy):
            part = {1: pl.ds(0, 4), 0: pl.ds(0, 8), -1: pl.ds(4, 4)}[dx]
            return src.at[part], dst.at[n, part]

        return exchange(kind, make)

    def assemble(own, got, out):
        for i in range(16):
            px = -1 if i < 4 else (0 if i < 12 else 1)
            r = i - 4 * px - 4
            for py, part in ((-1, slice(0, 8)), (1, slice(8, 16)), (0, slice(4, 12))):
                out[i, part] = own[r] if (px, py) == (0, 0) else got[from_source(px, py), r]

    def pre_level1(c):
        lv1.first_zero(0, 24)
        lv1.second_zero(0, 24)

        def store(i, n, r):
            m["r1"][pl.ds(i - 4, n)] = r

        lv1.residual(4, 20, store)
        small = []
        for i in range(8):
            total = jnp.zeros(tile_shape, F32)
            for q in range(2):
                for j in range(2):
                    total = total + m["r1"][2 * i + q, pl.ds(4 + j, 8, stride=2), :]
            small.append((zpair(total, 2) * 0.125)[None])
        g = jnp.concatenate(small, axis=0)
        m["g2t"][c] = g
        scr = m["s2t"][...]
        inv = m["i2t"][...]
        zero = jnp.zeros((1, 8, 128), F32)

        def image(v):
            up = jnp.concatenate([v[1:], zero], axis=0)
            dn = jnp.concatenate([zero, v[:-1]], axis=0)
            return (6.0 * v - side_sum(v, up, dn, 4)) * 0.0625 + scr * v

        v = g * inv * C1
        v = v + (CA * v + CB * ((g - image(v)) * inv))
        r = g - image(v)
        parts = []
        for xi in range(2):
            t = r[2 + 2 * xi] + r[3 + 2 * xi]
            t = zpair(t + roll(t, 7, 0), 4) * 0.125
            parts.append([t[2:3], t[4:5]])
        m["tile"][c] = pack3(parts)

    def dot(a, b):
        t = jnp.sum(a * b, axis=0)
        t = jnp.sum(t, axis=0, keepdims=True)
        return jnp.sum(t, axis=1, keepdims=True)[None]

    full = (half, 8, 128)
    lane3 = lanes(full)
    sub3 = rows(full)

    def image3(f, scr):
        left = roll(f, 126, 2)
        right = roll(f, 2, 2)
        after = jnp.where((lane & 4) == 0, left[0], 0.0)[None]
        ahead = jnp.where((lane & 4) != 0, right[half - 1], 0.0)[None]
        nxt = jnp.concatenate([right[1:], after], axis=0)
        prv = jnp.concatenate([ahead, left[:-1]], axis=0)
        total = jnp.where((lane3 & 2) == 0, left + prv, right + nxt)
        near = roll(f, 127, 2)
        far = roll(f, 1, 2)
        up = jnp.where(sub3 > 0, roll(near, 1, 1), 0.0)
        dn = jnp.where(sub3 < ngy - 1, roll(far, 7, 1), 0.0)
        total = total + jnp.where((lane3 & 1) == 0, near + up, far + dn)
        total = total + jnp.where(lane3 < 8, 0.0, roll(f, 8, 2))
        total = total + jnp.where(lane3 >= 120, 0.0, roll(f, 120, 2))
        q = (6.0 * f - total) * 0.015625 + scr * f
        return q if ngy == 8 else jnp.where(sub3 < ngy, q, 0.0)

    def coarse(g):
        scr = m["s3"][...]
        x = jnp.zeros(full, F32)
        r, p = g, g
        rr = dot(r, r)
        for it in range(COARSE_ITERS):
            q = image3(p, scr)
            alpha = rr / dot(p, q)
            x = x + alpha * p
            if it + 1 < COARSE_ITERS:
                r = r - alpha * q
                new = dot(r, r)
                p = r + (new / rr) * p
                rr = new
        m["e3"][...] = x

    first = (lane & 7) == 0

    def spread(v):
        v = jnp.where(first, v, 0.0)
        v = v + roll(v, 1, 1)
        v = v + roll(v, 2, 1)
        return v + roll(v, 4, 1)

    def post_level2():
        for a in range(-2, 3):
            at = wrap_x(gx + a)
            b = at // half
            t = m["e3"][at - b * half]
            t = roll(t, lax.rem(10 - gy, 8), 0)
            for xi in range(2):
                k = 2 * a + xi + 3
                if not 0 <= k < 8:
                    continue
                u = roll(t, 128 - 2 * xi - 4 * b, 1) if xi else roll(t, lax.rem(128 - 4 * b, 128), 1)
                even = spread(u)[1:5]
                odd_ = spread(roll(u, 127, 1))[0:4]
                m["pe2"][k, pl.ds(0, 4, stride=4), :] = odd_
                m["pe2"][k, pl.ds(1, 4, stride=4), :] = odd_
                m["pe2"][k, pl.ds(2, 4, stride=4), :] = even
                m["pe2"][k, pl.ds(3, 4, stride=4), :] = even
        for i in range(16):
            m["y2"][i + 1] = m["y2"][i + 1] + jnp.where(m["i2"][i] != 0.0, m["pe2"][i // 2], 0.0)
        lv2.pass_one(0, 16)
        lv2.pass_two(0, 16)

    def post_level1(c):
        for k in range(3, 13):
            e = m["y2"][k + 1, 2:14]
            m["pe1"][k, pl.ds(0, 12, stride=2), :] = e
            m["pe1"][k, pl.ds(1, 12, stride=2), :] = e
        lo, hi = ((2, 22), (4, 20))[c]

        def add(k):
            e = m["pe1"][k + 2]
            for q in range(2):
                m["y1"][2 * k + q + 1] = m["y1"][2 * k + q + 1] + e

        sweep(lo // 2, hi // 2, 1, add)
        lv1.pass_one(lo, hi)
        if c == 0:
            lv1.pass_two(4, 20)
        else:
            lv1.pass_two(6, 18)

    def post_level0(c):
        lo, hi = ((0, 32), (4, 28))[c]

        def build(k):
            e = m["y1"][k + 5, 4:20]
            m["pe0"][k, pl.ds(0, 16, stride=2), :] = e
            m["pe0"][k, pl.ds(1, 16, stride=2), :] = e

        def add(k):
            e = m["pe0"][k]
            for q in range(2):
                m["y0"][2 * k + q + 1] = m["y0"][2 * k + q + 1] + e

        sweep(lo // 2, hi // 2, 1, build)
        sweep(lo // 2, hi // 2, 1, add)
        lv0.pass_one(lo, hi)
        if c == 0:
            lv0.pass_two(2, 30)
        else:
            lv0.pass_two(lo, hi)

    for c in range(2):
        if c == 0:
            lv0.first_zero(0, 32)
            lv0.second_zero(0, 32)
        else:
            lv0.pass_one(4, 28)
            lv0.pass_two(4, 28)
        send_b(c)
        if c == 0:
            gather_two(2)
            setup_level1()
            copies_s2 = exchange_tile(EX_S2, m["s2t"], m["rs2"])
        take_b(c)
        pre_level1(c)
        gather_one(c)
        copies_g[c] = exchange_tile(EX_G + c, m["g2t"].at[c], m["rg2"].at[c])
        if c == 0:
            arrive(copies_s2)
            assemble(m["s2t"], m["rs2"], m["s2"])
            make_inv(lv2, 8, 16, 6)
        gather_two(c)
        arrive(copies_g[c])
        assemble(m["g2t"].at[c], m["rg2"].at[c], m["g2"])
        lv2.first_zero(0, 16)
        lv2.second_zero(0, 16)
        if c == 0:
            m["s3"][...] = gather_done(2)
        coarse(gather_done(c))
        post_level2()
        post_level1(c)
        post_level0(c)

    def store(i, n, r):
        res_ref[pl.ds(i - 8, n)] = r[:, 8:24]
        sol_ref[pl.ds(i - 8, n)] = m["y0"][pl.ds(i + 1, n), 8:24]

    lv0.residual(8, 24, store)

    for copy in sent:
        copy.wait_send()
    for c in range(3):
        wait_bytes(m["p1"].at[c, pl.ds(0, ngy - 1)], m["ags"].at[c, 0])
        wait_bytes(m["agb"].at[c, pl.ds(0, ngx - 1)], m["ags"].at[c, 2])


def solution(mesh):
    ngx, ngy = mesh.shape["gx"], mesh.shape["gy"]
    items = scratch_list(ngx)
    names = tuple(name for name, _ in items)

    def per_device(point_counts, face_counts):
        shape = jax.ShapeDtypeStruct(point_counts.shape, F32)
        return pl.pallas_call(
            functools.partial(kernel, ngx, ngy, names),
            out_shape=(shape, shape),
            in_specs=[pl.BlockSpec(memory_space=pl.ANY)] * 2,
            out_specs=(pl.BlockSpec(memory_space=pltpu.VMEM),) * 2,
            scratch_shapes=[spec for _, spec in items],
            compiler_params=pltpu.CompilerParams(
                collective_id=0, has_side_effects=True, vmem_limit_bytes=48 * 1024 * 1024
            ),
            name="poisson",
        )(point_counts, face_counts)

    return jax.shard_map(
        per_device,
        mesh=mesh,
        in_specs=(P("gx", "gy", None), P(None, "gx", "gy", None)),
        out_specs=(P("gx", "gy", None), P("gx", "gy", None)),
        check_vma=False,
    )
```

```python
import functools

import jax
import jax.numpy as jnp
from jax import lax
from jax.experimental import pallas as pl
from jax.experimental.pallas import tpu as pltpu
from jax.sharding import PartitionSpec as P


MESH = pl.DeviceIdType.MESH
F32 = jnp.float32
BF16 = jnp.bfloat16
NEIGH = ((-1, -1), (-1, 1), (1, -1), (1, 1), (-1, 0), (1, 0), (0, -1), (0, 1))

CENTRE = 0.5 * (2.0 + 0.3)
RADIUS = 0.5 * (2.0 - 0.3)
RATIO = CENTRE / RADIUS
MOM = 1.0 / RATIO
MOM2 = 1.0 / (2.0 * RATIO - MOM)
C1 = 1.0 / CENTRE
CA = MOM2 * MOM
CB = 2.0 * MOM2 / RADIUS
K0 = 1.0 - C1
K1 = 1.0 + CA - CB
K2 = CB / C1
COARSE_ITERS = 6


def lanes(shape):
    return lax.broadcasted_iota(jnp.int32, shape, len(shape) - 1)


def rows(shape):
    return lax.broadcasted_iota(jnp.int32, shape, len(shape) - 2)


def roll(v, shift, axis):
    return pltpu.roll(v, shift, axis)


def zpair(v, width):
    axis = v.ndim - 1
    low = (lanes(v.shape) & width) == 0
    return v + jnp.where(low, roll(v, 128 - width, axis), roll(v, width, axis))


def side_sum(c, up, dn, shift):
    ax = c.ndim - 2
    count = c.shape[ax]
    lane = lanes(c.shape)
    total = up + dn
    total = total + (roll(c, 1, ax) + roll(c, count - 1, ax))
    low = jnp.where(lane < shift, 0.0, roll(c, shift, ax + 1))
    high = jnp.where(lane >= 128 - shift, 0.0, roll(c, 128 - shift, ax + 1))
    return total + (low + high)


def sweep(lo, hi, step, body):
    def one(k, carry):
        body(lo + k * step)
        return carry

    lax.fori_loop(0, (hi - lo) // step, one, 0)


class Level:
    def __init__(self, x, y, g, w, dg, depth, step):
        self.x, self.y, self.g, self.w, self.dg = x, y, g, w, dg
        self.depth = depth
        self.shift = 2**depth
        self.step = step

    def around(self, src, i, n):
        c = src[pl.ds(i + 1, n)]
        total = side_sum(c, src[pl.ds(i + 2, n)], src[pl.ds(i, n)], self.shift)
        return c, total + self.g[pl.ds(i, n)]

    def first_zero(self, lo, hi):
        n = self.step

        def body(i):
            self.x[pl.ds(i + 1, n)] = self.g[pl.ds(i, n)] * self.w[pl.ds(i, n)]

        sweep(lo, hi, n, body)

    def second_zero(self, lo, hi):
        n = self.step

        def body(i):
            c, t = self.around(self.x, i, n)
            self.y[pl.ds(i + 1, n)] = K1 * c + K2 * (t * self.w[pl.ds(i, n)])

        sweep(lo, hi, n, body)

    def pass_one(self, lo, hi):
        n = self.step

        def body(i):
            c, t = self.around(self.y, i, n)
            self.x[pl.ds(i + 1, n)] = K0 * c + t * self.w[pl.ds(i, n)]

        sweep(lo, hi, n, body)

    def pass_two(self, lo, hi):
        n = self.step

        def body(i):
            c, t = self.around(self.x, i, n)
            old = self.y[pl.ds(i + 1, n)]
            self.y[pl.ds(i + 1, n)] = (K1 * c - CA * old) + K2 * (t * self.w[pl.ds(i, n)])

        sweep(lo, hi, n, body)

    def residual(self, lo, hi, store):
        n = self.step

        def body(i):
            c, t = self.around(self.y, i, n)
            store(i, n, t - self.dg[pl.ds(i, n)] * c)

        sweep(lo, hi, n, body)


def scratch_list(ngx):
    v = pltpu.VMEM
    return (
        ("fcv", v((3, 16, 16, 128), jnp.int32)),
        ("pcv", v((16, 16, 128), jnp.int32)),
        ("ext", v((32, 4, 16, 128), BF16)),
        ("exs", v((2, 16, 128), BF16)),
        ("rex", v((8, 2, 16, 128), BF16)),
        ("s1p", v((4, 16, 128), BF16)),
        ("rs1", v((8, 4, 16, 128), BF16)),
        ("scrown", v((16, 16, 128), F32)),
        ("s1own", v((8, 8, 128), F32)),
        ("fy1", v((32, 128), F32)),
        ("fy2", v((32, 128), F32)),
        ("x0", v((34, 32, 128), F32)),
        ("y0", v((34, 32, 128), F32)),
        ("g0", v((32, 32, 128), F32)),
        ("w0", v((32, 32, 128), F32)),
        ("dg0", v((32, 32, 128), F32)),
        ("r0", v((16, 16, 128), F32)),
        ("pk", v((2, 4, 8, 128), F32)),
        ("rb", v((2, 8, 4, 8, 128), F32)),
        ("x1", v((26, 24, 128), F32)),
        ("y1", v((26, 24, 128), F32)),
        ("g1", v((24, 24, 128), F32)),
        ("s1", v((24, 24, 128), F32)),
        ("w1", v((24, 24, 128), F32)),
        ("dg1", v((24, 24, 128), F32)),
        ("r1", v((16, 24, 128), F32)),
        ("s2t", v((8, 8, 128), F32)),
        ("w2t", v((8, 8, 128), F32)),
        ("rs2", v((8, 8, 8, 128), F32)),
        ("g2t", v((2, 8, 8, 128), F32)),
        ("rg2", v((2, 8, 8, 8, 128), F32)),
        ("x2", v((18, 16, 128), F32)),
        ("y2", v((18, 16, 128), F32)),
        ("g2", v((16, 16, 128), F32)),
        ("s2", v((16, 16, 128), F32)),
        ("w2", v((16, 16, 128), F32)),
        ("dg2", v((16, 16, 128), F32)),
        ("pe2", v((8, 16, 128), F32)),
        ("tile", v((3, 4, 128), F32)),
        ("p1", v((3, 7, 4, 128), F32)),
        ("agb", v((3, ngx, 4, 128), F32)),
        ("dg3", v((ngx // 2, 8, 128), F32)),
        ("e3", v((ngx // 2, 8, 128), F32)),
        ("snd", pltpu.SemaphoreType.DMA((8, 8))),
        ("rcv", pltpu.SemaphoreType.DMA((8, 8))),
        ("ags", pltpu.SemaphoreType.DMA((3, 4))),
        ("loc", pltpu.SemaphoreType.DMA((2,))),
    )


EX_IN, EX_FACE, EX_S1, EX_S2, EX_B, EX_G = 0, 1, 2, 3, 4, 6


def kernel(ngx, ngy, names, pc_hbm, fc_hbm, sol_ref, res_ref, *scratch):
    m = dict(zip(names, scratch))
    gx = lax.axis_index("gx")
    gy = lax.axis_index("gy")
    half = ngx // 2
    nx0, ny0 = 16 * ngx, 16 * ngy

    def wrap_x(v):
        return lax.rem(v + ngx, ngx)

    def wrap_y(v):
        return lax.rem(v + ngy, ngy)

    copy_p = pltpu.make_async_copy(pc_hbm, m["pcv"], m["loc"].at[0])
    copy_f = pltpu.make_async_copy(fc_hbm, m["fcv"], m["loc"].at[1])
    copy_p.start()
    copy_f.start()

    barrier = pltpu.get_barrier_semaphore()
    peers = 0
    for o in range(1, ngy):
        pl.semaphore_signal(barrier, inc=1, device_id=(gx, wrap_y(gy + o)), device_id_type=MESH)
        peers += 1

    def greet(o, carry):
        pl.semaphore_signal(barrier, inc=1, device_id=(wrap_x(gx + o), gy), device_id_type=MESH)
        return carry

    lax.fori_loop(1, ngx, greet, 0)
    peers += ngx - 1
    for dx, dy in NEIGH:
        if dx != 0 and dy != 0:
            pl.semaphore_signal(
                barrier, inc=1, device_id=(wrap_x(gx + dx), wrap_y(gy + dy)), device_id_type=MESH
            )
            peers += 1

    for name in ("x0", "y0", "x1", "y1", "x2", "y2"):
        ref = m[name]
        last = ref.shape[0] - 1
        ref[0] = jnp.zeros(ref.shape[1:], F32)
        ref[last] = jnp.zeros(ref.shape[1:], F32)

    spans = {1: (8, 8, 0), 0: (0, 16, 8), -1: (0, 8, 24)}
    tiles = {1: (1, 1, 0), 0: (0, 2, 1), -1: (0, 1, 3)}

    def exists(dx, dy):
        x, y = gx + dx, gy + dy
        return (x >= 0) & (x < ngx) & (y >= 0) & (y < ngy)

    for n, (dx, dy) in enumerate(NEIGH):

        @pl.when(jnp.logical_not(exists(-dx, -dy)))
        def _():
            _, xn, xd = spans[dx]
            _, yn, yd = tiles[dy]
            m["ext"][xd : xd + xn, yd : yd + yn] = jnp.zeros((xn, yn, 16, 128), BF16)
            for name in ("rex", "rs1", "rs2"):
                m[name][n] = jnp.zeros(m[name].shape[1:], m[name].dtype)
            for name in ("rb", "rg2"):
                for c in range(2):
                    m[name][c, n] = jnp.zeros(m[name].shape[2:], F32)

    copy_f.wait()
    copy_p.wait()
    fcv, pcv = m["fcv"], m["pcv"]

    def own_rows(i):
        def counts(d, at, n):
            return fcv[d, pl.ds(at, n)].astype(F32) * 0.125

        f0, f1, f2 = counts(0, i, 4), counts(1, i, 4), counts(2, i, 4)
        before = jnp.where(i > 0, counts(0, jnp.maximum(i - 1, 0), 1), 0.0)
        low_x = jnp.concatenate([before, f0[:3]], axis=0)
        low_y = jnp.where(rows(f1.shape) == 0, 0.0, roll(f1, 1, 1))
        low_z = jnp.where(lanes(f2.shape) == 0, 0.0, roll(f2, 1, 2))
        src = (low_x - f0) + (low_y - f1) + (low_z - f2)
        scr = pcv[pl.ds(i, 4)].astype(F32) * 0.25
        m["scrown"][pl.ds(i, 4)] = scr
        for t in range(2):
            part = slice(8 * t, 8 * t + 8)
            m["ext"][pl.ds(i + 8, 4), t + 1] = jnp.concatenate([src[:, part], scr[:, part]], axis=1).astype(BF16)

    sweep(0, 16, 4, own_rows)

    tile_shape = (8, 128)
    sub = rows(tile_shape)
    lane = lanes(tile_shape)
    face_x = fcv[0, 15].astype(F32) * 0.125
    own_fx = [face_x[0:8], face_x[8:16]]
    own_fy = []
    for h in range(2):
        total = jnp.zeros(tile_shape, F32)
        for r in range(8):
            row = fcv[1, 8 * h + r, 15:16].astype(F32) * 0.125
            total = jnp.where(sub == r, row, total)
        own_fy.append(total)
    for t in range(2):
        m["exs"][t] = jnp.concatenate([own_fx[t], own_fy[t]], axis=0).astype(BF16)

    pl.semaphore_wait(barrier, peers)

    sent = []

    def exchange(kind, make):
        copies = []
        for n, (dx, dy) in enumerate(NEIGH):
            src, dst = make(n, dx, dy)
            copy = pltpu.make_async_remote_copy(
                src_ref=src,
                dst_ref=dst,
                send_sem=m["snd"].at[kind, n],
                recv_sem=m["rcv"].at[kind, n],
                device_id=(wrap_x(gx + dx), wrap_y(gy + dy)),
                device_id_type=MESH,
            )
            pl.when(exists(dx, dy))(copy.start)
            copies.append(copy)
        sent.append(copies)
        return copies

    def arrive(copies):
        for copy, (dx, dy) in zip(copies, NEIGH):
            pl.when(exists(-dx, -dy))(copy.wait_recv)

    def from_source(px, py):
        return NEIGH.index((-px, -py))

    def make_in(n, dx, dy):
        xs, xn, xd = spans[dx]
        ys, yn, yd = tiles[dy]
        src = m["ext"].at[pl.ds(xs + 8, xn), pl.ds(ys + 1, yn)]
        dst = m["ext"].at[pl.ds(xd, xn), pl.ds(yd, yn)]
        return src, dst

    copies_face = exchange(EX_FACE, lambda n, dx, dy: (m["exs"], m["rex"].at[n]))
    copies_in = exchange(EX_IN, make_in)

    own1 = []
    for i in range(8):
        total = jnp.zeros(tile_shape, F32)
        for q in range(2):
            for j in range(2):
                total = total + m["scrown"][2 * i + q, pl.ds(j, 8, stride=2), :]
        v = zpair(total, 1) * 0.125
        m["s1own"][i] = v
        own1.append(v)
    for k in range(4):
        m["s1p"][k] = jnp.concatenate([own1[2 * k], own1[2 * k + 1]], axis=0).astype(BF16)
    copies_s1 = exchange(EX_S1, lambda n, dx, dy: (m["s1p"], m["rs1"].at[n]))

    own3 = []
    for xi in range(2):
        pair = jnp.zeros((4, 128), F32)
        for q in range(2):
            quad = jnp.zeros((4, 128), F32)
            for h in range(2):
                for j in range(2):
                    quad = quad + m["s1own"][4 * xi + 2 * q + h, pl.ds(j, 4, stride=2), :]
            pair = pair + zpair(quad, 2) * 0.125
        pair = zpair(pair, 4) * 0.125
        own3 += [pair[0:1] + pair[1:2], pair[2:3] + pair[3:4]]
    m["tile"][2] = jnp.concatenate(own3, axis=0)

    def gather_one(c):
        for o in range(1, ngy):
            pltpu.make_async_remote_copy(
                src_ref=m["tile"].at[c],
                dst_ref=m["p1"].at[c, o - 1],
                send_sem=m["ags"].at[c, 0],
                recv_sem=m["ags"].at[c, 1],
                device_id=(gx, wrap_y(gy + o)),
                device_id_type=MESH,
            ).start()

    def wait_bytes(ref, sem):
        pltpu.make_async_copy(ref, ref, sem).wait()

    def gather_two(c):
        wait_bytes(m["p1"].at[c, pl.ds(0, ngy - 1)], m["ags"].at[c, 1])
        slot = lanes((4, 128)) & 7
        total = jnp.where(slot == gy, m["tile"][c], 0.0)
        for o in range(1, ngy):
            total = jnp.where(slot == wrap_y(gy - o), m["p1"][c, o - 1], total)
        m["agb"][c, gx] = total

        def send(o, carry):
            pltpu.make_async_remote_copy(
                src_ref=m["agb"].at[c, gx],
                dst_ref=m["agb"].at[c, gx],
                send_sem=m["ags"].at[c, 2],
                recv_sem=m["ags"].at[c, 3],
                device_id=(wrap_x(gx + o), gy),
                device_id_type=MESH,
            ).start()
            return carry

        lax.fori_loop(1, ngx, send, 0)

    def gather_done(c):
        wait_bytes(m["agb"].at[c, pl.ds(0, ngx - 1)], m["ags"].at[c, 3])
        return jnp.concatenate([m["agb"][c, 0:half], m["agb"][c, half:ngx]], axis=1)

    gather_one(2)

    arrive(copies_face)
    gate_x = jnp.where(gx > 0, 1.0, 0.0)
    gate_y = jnp.where(gy > 0, 1.0, 0.0)

    def face(px, py, t):
        return m["rex"][from_source(px, py), t].astype(F32)

    m["fy1"][0:8] = face(-1, -1, 1)[8:16] * gate_y
    m["fy1"][8:16] = face(0, -1, 0)[8:16] * gate_y
    m["fy1"][16:24] = face(0, -1, 1)[8:16] * gate_y
    m["fy1"][24:32] = face(1, -1, 0)[8:16] * gate_y
    m["fy2"][0:8] = face(-1, 0, 1)[8:16]
    m["fy2"][8:16] = own_fy[0]
    m["fy2"][16:24] = own_fy[1]
    m["fy2"][24:32] = face(1, 0, 0)[8:16]
    arrive(copies_in)

    def inside(shape, i, level, off):
        x = lax.broadcasted_iota(jnp.int32, shape, 0) + (i - off + gx * (16 >> level))
        y = rows(shape) + (gy * (16 >> level) - off)
        return (x >= 0) & (x < (nx0 >> level)) & (y >= 0) & (y < (ny0 >> level))

    def weight(dg, i, level, off):
        return jnp.where(inside(dg.shape, i, level, off), C1 / dg, 0.0)

    def unpack_in(i):
        n = 2
        for t in range(4):
            part = slice(8 * t, 8 * t + 8)
            pair = m["ext"][pl.ds(i, n), t].astype(F32)
            src = pair[:, 0:8]
            if t % 2 == 1:
                edge = m["fy1" if t == 1 else "fy2"]
                src = jnp.concatenate(
                    [(src[q] + jnp.where(sub == 0, edge[pl.ds(i + q, 1)], 0.0))[None] for q in range(n)], axis=0
                )
            dg = 6.0 + pair[:, 8:16]
            x = lax.broadcasted_iota(jnp.int32, dg.shape, 0) + (i - 8 + gx * 16)
            y = rows(dg.shape) + (gy * 16 - 8 + 8 * t)
            mask = (x >= 0) & (x < nx0) & (y >= 0) & (y < ny0)
            w = jnp.where(mask, C1 / dg, 0.0)
            m["g0"][pl.ds(i, n), part] = src
            m["dg0"][pl.ds(i, n), part] = dg
            m["w0"][pl.ds(i, n), part] = w
            m["x0"][pl.ds(i + 1, n), part] = src * w

    sweep(0, 32, 2, unpack_in)
    for t, (py, k) in enumerate(((-1, 1), (0, 0), (0, 1), (1, 0))):
        part = slice(8 * t, 8 * t + 8)
        upper = own_fx[k] if py == 0 else face(0, py, k)[0:8]
        for at, extra in ((8, face(-1, py, k)[0:8] * gate_x), (24, upper)):
            total = m["g0"][at, part] + extra
            m["g0"][at, part] = total
            m["x0"][at + 1, part] = total * m["w0"][at, part]

    lv0 = Level(m["x0"], m["y0"], m["g0"], m["w0"], m["dg0"], 0, 4)
    lv1 = Level(m["x1"], m["y1"], m["g1"], m["w1"], m["dg1"], 1, 4)
    lv2 = Level(m["x2"], m["y2"], m["g2"], m["w2"], m["dg2"], 2, 16)

    def make_weights(level, scr, step, count, off):
        def body(i):
            dg = 6.0 + scr[pl.ds(i, step)] * float(4**level.depth)
            level.dg[pl.ds(i, step)] = dg
            level.w[pl.ds(i, step)] = weight(dg, i, level.depth, off)

        sweep(0, count, step, body)

    odd = (lane & 1) == 1
    copies_b = [None, None]
    copies_g = [None, None]

    def send_b(c):
        def store(i, n, r):
            m["r0"][pl.ds(i - 8, n)] = r[:, 8:24]

        lv0.residual(8, 24, store)
        fine = []
        for i in range(8):
            total = jnp.zeros(tile_shape, F32)
            for q in range(2):
                for j in range(2):
                    total = total + m["r0"][2 * i + q, pl.ds(j, 8, stride=2), :]
            v = zpair(total, 1) * 0.5
            m["g1"][8 + i, 8:16] = v
            fine.append(v)
        for k in range(4):
            m["pk"][c, k] = jnp.where(odd, fine[2 * k + 1], fine[2 * k])

        def make(n, dx, dy):
            count = 4 if dx == 0 or (c == 0 and dy == 0) else 3
            part = pl.ds(4 - count if dx == 1 else 0, count)
            return m["pk"].at[c, part], m["rb"].at[c, n, part]

        copies_b[c] = exchange(EX_B + c, make)

    def take_b(c):
        arrive(copies_b[c])
        for n, (dx, dy) in enumerate(NEIGH):
            base = 8 - 8 * dx
            part = slice(8 - 8 * dy, 16 - 8 * dy)
            ks = range(4) if dx == 0 or (c == 0 and dy == 0) else (range(1, 4) if dx == 1 else range(3))
            for k in ks:
                v = m["rb"][c, n, k]
                m["g1"][base + 2 * k, part] = jnp.where(odd, roll(v, 1, 1), v)
                m["g1"][base + 2 * k + 1, part] = jnp.where(odd, v, roll(v, 127, 1))

    def setup_level1():
        arrive(copies_s1)
        for i in range(8):
            m["s1"][8 + i, 8:16] = m["s1own"][i]
        for n, (dx, dy) in enumerate(NEIGH):
            base = 8 - 8 * dx
            part = slice(8 - 8 * dy, 16 - 8 * dy)
            for k in range(4):
                v = m["rs1"][n, k].astype(F32)
                m["s1"][base + 2 * k, part] = v[0:8]
                m["s1"][base + 2 * k + 1, part] = v[8:16]
        make_weights(lv1, m["s1"], 4, 24, 8)
        for i in range(8):
            total = jnp.zeros(tile_shape, F32)
            for q in range(2):
                for j in range(2):
                    total = total + m["s1"][4 + 2 * i + q, pl.ds(4 + j, 8, stride=2), :]
            m["s2t"][i] = zpair(total, 2) * 0.125
        m["w2t"][...] = weight(6.0 + m["s2t"][...] * 16.0, 0, 2, 2)

    def exchange_tile(kind, src, dst):
        def make(n, dx, dy):
            part = {1: pl.ds(0, 4), 0: pl.ds(0, 8), -1: pl.ds(4, 4)}[dx]
            return src.at[part], dst.at[n, part]

        return exchange(kind, make)

    def assemble(own, got, out):
        for i in range(16):
            px = -1 if i < 4 else (0 if i < 12 else 1)
            r = i - 4 * px - 4
            for py, part in ((-1, slice(0, 8)), (1, slice(8, 16)), (0, slice(4, 12))):
                out[i, part] = own[r] if (px, py) == (0, 0) else got[from_source(px, py), r]

    def pre_level1(c):
        lv1.first_zero(0, 24)
        lv1.second_zero(0, 24)

        def store(i, n, r):
            m["r1"][pl.ds(i - 4, n)] = r

        lv1.residual(4, 20, store)
        small = []
        for i in range(8):
            total = jnp.zeros(tile_shape, F32)
            for q in range(2):
                for j in range(2):
                    total = total + m["r1"][2 * i + q, pl.ds(4 + j, 8, stride=2), :]
            small.append((zpair(total, 2) * 0.5)[None])
        g = jnp.concatenate(small, axis=0)
        m["g2t"][c] = g
        dg = 6.0 + m["s2t"][...] * 16.0
        w = m["w2t"][...]
        zero = jnp.zeros((1, 8, 128), F32)

        def around(v):
            up = jnp.concatenate([v[1:], zero], axis=0)
            dn = jnp.concatenate([zero, v[:-1]], axis=0)
            return g + side_sum(v, up, dn, 4)

        v = g * w
        v = K1 * v + K2 * (around(v) * w)
        r = around(v) - dg * v
        parts = []
        for xi in range(2):
            t = r[2 + 2 * xi] + r[3 + 2 * xi]
            t = zpair(t + roll(t, 7, 0), 4) * 0.5
            parts += [t[2:3], t[4:5]]
        m["tile"][c] = jnp.concatenate(parts, axis=0)

    def dot(a, b):
        t = jnp.sum(a * b, axis=0)
        t = jnp.sum(t, axis=0, keepdims=True)
        return jnp.sum(t, axis=1, keepdims=True)[None]

    full = (half, 8, 128)
    lane3 = lanes(full)
    sub3 = rows(full)
    slot3 = lane3 & 7
    even_y = (sub3 & 1) == 0
    even_x = (sub3 & 2) == 0
    low_y = even_y & (slot3 > 0)
    high_y = jnp.logical_not(even_y) & (slot3 < ngy - 1)

    def image3(f, dg):
        swap = jnp.where(even_y, roll(f, 7, 1), roll(f, 1, 1))
        total = swap + jnp.where(low_y, roll(swap, 1, 2), jnp.where(high_y, roll(swap, 127, 2), 0.0))
        left = roll(f, 6, 1)
        right = roll(f, 2, 1)
        after = jnp.where(sub < 4, left[0], 0.0)[None]
        ahead = jnp.where(sub >= 4, right[half - 1], 0.0)[None]
        nxt = jnp.concatenate([right[1:], after], axis=0)
        prv = jnp.concatenate([ahead, left[:-1]], axis=0)
        total = total + jnp.where(even_x, left + prv, right + nxt)
        total = total + jnp.where(lane3 < 8, 0.0, roll(f, 8, 2))
        total = total + jnp.where(lane3 >= 120, 0.0, roll(f, 120, 2))
        q = dg * f - total
        return q if ngy == 8 else jnp.where(slot3 < ngy, q, 0.0)

    def coarse(r):
        dg = m["dg3"][...]
        x = p = q = rr_old = curve = None
        for it in range(COARSE_ITERS):
            image = image3(r, dg)
            rr = dot(r, r)
            rar = dot(r, image)
            if it == 0:
                p, q, curve = r, image, rar
            else:
                beta = rr / rr_old
                curve = rar - beta * beta * curve
                p = r + beta * p
                q = image + beta * q
            alpha = rr / curve
            x = alpha * p if it == 0 else x + alpha * p
            if it + 1 < COARSE_ITERS:
                r = r - alpha * q
            rr_old = rr
        m["e3"][...] = x

    step_y = (sub + 1) >> 1
    pick = (lane & 7) == step_y

    def post_level2():
        for k in range(8):
            a, xi = (k - 3) >> 1, (k - 3) & 1
            at = wrap_x(gx + a)
            b = at // half
            v = at - b * half
            low = m["e3"][v, pl.ds(4 * b + 2 * xi, 1)]
            high = m["e3"][v, pl.ds(4 * b + 2 * xi + 1, 1)]
            t = jnp.where((sub & 1) == 1, low, high)
            t = roll(t, lax.rem(130 - gy, 128), 1)
            t = jnp.where(pick, t, 0.0)
            for width in (4, 2, 1):
                t = jnp.where((step_y & width) != 0, roll(t, 128 - width, 1), t)
            for width in (1, 2, 4):
                t = t + roll(t, width, 1)
            m["pe2"][k, pl.ds(0, 8, stride=2), :] = t
            m["pe2"][k, pl.ds(1, 8, stride=2), :] = t
        for i in range(16):
            m["y2"][i + 1] = m["y2"][i + 1] + jnp.where(m["w2"][i] != 0.0, m["pe2"][i // 2], 0.0)
        lv2.pass_one(0, 16)
        lv2.pass_two(0, 16)

    def post_level1(c):
        lo, hi = ((2, 22), (4, 20))[c]
        for i in range(lo, hi):
            e = m["y2"][i // 2 + 3, 2:14]
            for j in range(2):
                at = pl.ds(j, 12, stride=2)
                m["y1"][i + 1, at, :] = m["y1"][i + 1, at, :] + e
        lv1.pass_one(lo, hi)
        if c == 0:
            lv1.pass_two(4, 20)
        else:
            lv1.pass_two(6, 18)

    def post_level0(c):
        lo, hi = ((0, 32), (4, 28))[c]

        def add(k):
            for h in range(2):
                e = m["y1"][k + h + 5, 4:20]
                for q in range(2):
                    for j in range(2):
                        at = pl.ds(j, 16, stride=2)
                        i = 2 * (k + h) + q + 1
                        m["y0"][i, at, :] = m["y0"][i, at, :] + e

        sweep(lo // 2, hi // 2, 2, add)
        lv0.pass_one(lo, hi)
        if c == 0:
            lv0.pass_two(2, 30)
        else:
            lv0.pass_two(lo, hi)

    for c in range(2):
        if c == 0:
            lv0.second_zero(0, 32)
        else:
            lv0.pass_one(4, 28)
            lv0.pass_two(4, 28)
        send_b(c)
        if c == 0:
            gather_two(2)
            setup_level1()
            copies_s2 = exchange_tile(EX_S2, m["s2t"], m["rs2"])
        take_b(c)
        pre_level1(c)
        gather_one(c)
        copies_g[c] = exchange_tile(EX_G + c, m["g2t"].at[c], m["rg2"].at[c])
        if c == 0:
            arrive(copies_s2)
            assemble(m["s2t"], m["rs2"], m["s2"])
            make_weights(lv2, m["s2"], 8, 16, 6)
        gather_two(c)
        arrive(copies_g[c])
        assemble(m["g2t"].at[c], m["rg2"].at[c], m["g2"])
        lv2.first_zero(0, 16)
        lv2.second_zero(0, 16)
        if c == 0:
            m["dg3"][...] = 6.0 + gather_done(2) * 64.0
        coarse(gather_done(c))
        post_level2()
        post_level1(c)
        post_level0(c)

    def store(i, n, r):
        res_ref[pl.ds(i - 8, n)] = r[:, 8:24]
        sol_ref[pl.ds(i - 8, n)] = m["y0"][pl.ds(i + 1, n), 8:24]

    lv0.residual(8, 24, store)

    for copies in sent:
        for copy, (dx, dy) in zip(copies, NEIGH):
            pl.when(exists(dx, dy))(copy.wait_send)
    for c in range(3):
        wait_bytes(m["p1"].at[c, pl.ds(0, ngy - 1)], m["ags"].at[c, 0])
        wait_bytes(m["agb"].at[c, pl.ds(0, ngx - 1)], m["ags"].at[c, 2])


def solution(mesh):
    ngx, ngy = mesh.shape["gx"], mesh.shape["gy"]
    items = scratch_list(ngx)
    names = tuple(name for name, _ in items)

    def per_device(point_counts, face_counts):
        shape = jax.ShapeDtypeStruct(point_counts.shape, F32)
        return pl.pallas_call(
            functools.partial(kernel, ngx, ngy, names),
            out_shape=(shape, shape),
            in_specs=[pl.BlockSpec(memory_space=pltpu.HBM)] * 2,
            out_specs=(pl.BlockSpec(memory_space=pltpu.VMEM),) * 2,
            scratch_shapes=[spec for _, spec in items],
            compiler_params=pltpu.CompilerParams(
                collective_id=0, has_side_effects=True, vmem_limit_bytes=48 * 1024 * 1024
            ),
            name="poisson",
        )(point_counts, face_counts)

    return jax.shard_map(
        per_device,
        mesh=mesh,
        in_specs=(P("gx", "gy", None), P(None, "gx", "gy", None)),
        out_specs=(P("gx", "gy", None), P("gx", "gy", None)),
        check_vma=False,
    )
```

```python
import functools

import jax
import jax.numpy as jnp
from jax import lax
from jax.experimental import pallas as pl
from jax.experimental.pallas import tpu as pltpu
from jax.sharding import PartitionSpec as P


MESH = pl.DeviceIdType.MESH
F32 = jnp.float32
BF16 = jnp.bfloat16
NEIGH = ((-1, -1), (-1, 1), (1, -1), (1, 1), (-1, 0), (1, 0), (0, -1), (0, 1))

CENTRE = 0.5 * (2.0 + 0.3)
RADIUS = 0.5 * (2.0 - 0.3)
RATIO = CENTRE / RADIUS
MOM = 1.0 / RATIO
MOM2 = 1.0 / (2.0 * RATIO - MOM)
C1 = 1.0 / CENTRE
CA = MOM2 * MOM
CB = 2.0 * MOM2 / RADIUS
K0 = 1.0 - C1
K1 = 1.0 + CA - CB
K2 = CB / C1
COARSE_ITERS = 6


def lanes(shape):
    return lax.broadcasted_iota(jnp.int32, shape, len(shape) - 1)


def rows(shape):
    return lax.broadcasted_iota(jnp.int32, shape, len(shape) - 2)


def roll(v, shift, axis):
    return pltpu.roll(v, shift, axis)


def zpair(v, width):
    axis = v.ndim - 1
    low = (lanes(v.shape) & width) == 0
    return v + jnp.where(low, roll(v, 128 - width, axis), roll(v, width, axis))


def side_sum(c, up, dn, shift):
    ax = c.ndim - 2
    count = c.shape[ax]
    lane = lanes(c.shape)
    total = up + dn
    total = total + (roll(c, 1, ax) + roll(c, count - 1, ax))
    low = jnp.where(lane < shift, 0.0, roll(c, shift, ax + 1))
    high = jnp.where(lane >= 128 - shift, 0.0, roll(c, 128 - shift, ax + 1))
    return total + (low + high)


def sweep(lo, hi, step, body):
    def one(k, carry):
        body(lo + k * step)
        return carry

    lax.fori_loop(0, (hi - lo) // step, one, 0, unroll=True)


class Level:
    def __init__(self, x, y, g, w, dg, depth):
        self.x, self.y, self.g, self.w, self.dg = x, y, g, w, dg
        self.depth = depth
        self.shift = 2**depth
        self.count = g.shape[1]
        self.mid = slice(8, 8 + self.count)

    def around(self, src, i, n):
        c = src[pl.ds(i + 1, n), self.mid]
        lane = lanes(c.shape)
        total = src[pl.ds(i + 2, n), self.mid] + src[pl.ds(i, n), self.mid]
        total = total + (src[pl.ds(i + 1, n), 7 : 7 + self.count] + src[pl.ds(i + 1, n), 9 : 9 + self.count])
        low = jnp.where(lane < self.shift, 0.0, roll(c, self.shift, 2))
        high = jnp.where(lane >= 128 - self.shift, 0.0, roll(c, 128 - self.shift, 2))
        return c, (total + self.g[pl.ds(i, n)]) + (low + high)

    def first_zero(self, lo, hi, n):
        def body(i):
            self.x[pl.ds(i + 1, n), self.mid] = self.g[pl.ds(i, n)] * self.w[pl.ds(i, n)]

        sweep(lo, hi, n, body)

    def second_zero(self, lo, hi, n):
        def body(i):
            c, t = self.around(self.x, i, n)
            self.y[pl.ds(i + 1, n), self.mid] = K1 * c + K2 * (t * self.w[pl.ds(i, n)])

        sweep(lo, hi, n, body)

    def pass_one(self, lo, hi, n):
        def body(i):
            c, t = self.around(self.y, i, n)
            self.x[pl.ds(i + 1, n), self.mid] = K0 * c + t * self.w[pl.ds(i, n)]

        sweep(lo, hi, n, body)

    def pass_two(self, lo, hi, n):
        def body(i):
            c, t = self.around(self.x, i, n)
            old = self.y[pl.ds(i + 1, n), self.mid]
            self.y[pl.ds(i + 1, n), self.mid] = (K1 * c - CA * old) + K2 * (t * self.w[pl.ds(i, n)])

        sweep(lo, hi, n, body)

    def residual(self, lo, hi, n, store):
        def body(i):
            c, t = self.around(self.y, i, n)
            store(i, n, t - self.dg[pl.ds(i, n)] * c)

        sweep(lo, hi, n, body)


def scratch_list(ngx):
    v = pltpu.VMEM
    return (
        ("fcv", v((3, 16, 16, 128), jnp.int32)),
        ("pcv", v((16, 16, 128), jnp.int32)),
        ("ext", v((32, 4, 16, 128), BF16)),
        ("exs", v((2, 16, 128), BF16)),
        ("rex", v((8, 2, 16, 128), BF16)),
        ("s1p", v((4, 16, 128), BF16)),
        ("rs1", v((8, 4, 16, 128), BF16)),
        ("scrown", v((16, 16, 128), F32)),
        ("s1own", v((8, 8, 128), F32)),
        ("fy1", v((32, 128), F32)),
        ("fy2", v((32, 128), F32)),
        ("x0", v((34, 48, 128), F32)),
        ("y0", v((34, 48, 128), F32)),
        ("g0", v((32, 32, 128), F32)),
        ("w0", v((32, 32, 128), F32)),
        ("dg0", v((32, 32, 128), F32)),
        ("r0", v((16, 16, 128), F32)),
        ("pk", v((2, 4, 8, 128), F32)),
        ("rb", v((2, 8, 4, 8, 128), F32)),
        ("x1", v((26, 40, 128), F32)),
        ("y1", v((26, 40, 128), F32)),
        ("g1", v((24, 24, 128), F32)),
        ("s1", v((24, 24, 128), F32)),
        ("w1", v((24, 24, 128), F32)),
        ("dg1", v((24, 24, 128), F32)),
        ("r1", v((16, 24, 128), F32)),
        ("s2t", v((8, 8, 128), F32)),
        ("w2t", v((8, 8, 128), F32)),
        ("rs2", v((8, 8, 8, 128), F32)),
        ("g2t", v((2, 8, 8, 128), F32)),
        ("rg2", v((2, 8, 8, 8, 128), F32)),
        ("x2", v((18, 32, 128), F32)),
        ("y2", v((18, 32, 128), F32)),
        ("g2", v((16, 16, 128), F32)),
        ("s2", v((16, 16, 128), F32)),
        ("w2", v((16, 16, 128), F32)),
        ("dg2", v((16, 16, 128), F32)),
        ("pe2", v((8, 16, 128), F32)),
        ("tile", v((3, 4, 128), F32)),
        ("p1", v((3, 7, 4, 128), F32)),
        ("agb", v((3, ngx, 4, 128), F32)),
        ("dg3", v((ngx // 2, 8, 128), F32)),
        ("e3", v((ngx // 2, 8, 128), F32)),
        ("snd", pltpu.SemaphoreType.DMA((8, 8))),
        ("rcv", pltpu.SemaphoreType.DMA((8, 8))),
        ("ags", pltpu.SemaphoreType.DMA((3, 4))),
        ("loc", pltpu.SemaphoreType.DMA((2,))),
    )


EX_IN, EX_FACE, EX_S1, EX_S2, EX_B, EX_G = 0, 1, 2, 3, 4, 6


def kernel(ngx, ngy, names, pc_hbm, fc_hbm, sol_ref, res_ref, *scratch):
    m = dict(zip(names, scratch))
    gx = lax.axis_index("gx")
    gy = lax.axis_index("gy")
    half = ngx // 2
    nx0, ny0 = 16 * ngx, 16 * ngy

    def wrap_x(v):
        return lax.rem(v + ngx, ngx)

    def wrap_y(v):
        return lax.rem(v + ngy, ngy)

    copy_p = pltpu.make_async_copy(pc_hbm, m["pcv"], m["loc"].at[0])
    copy_f = pltpu.make_async_copy(fc_hbm, m["fcv"], m["loc"].at[1])
    copy_p.start()
    copy_f.start()

    barrier = pltpu.get_barrier_semaphore()
    peers = 0
    for o in range(1, ngy):
        pl.semaphore_signal(barrier, inc=1, device_id=(gx, wrap_y(gy + o)), device_id_type=MESH)
        peers += 1

    def greet(o, carry):
        pl.semaphore_signal(barrier, inc=1, device_id=(wrap_x(gx + o), gy), device_id_type=MESH)
        return carry

    lax.fori_loop(1, ngx, greet, 0)
    peers += ngx - 1
    for dx, dy in NEIGH:
        if dx != 0 and dy != 0:
            pl.semaphore_signal(
                barrier, inc=1, device_id=(wrap_x(gx + dx), wrap_y(gy + dy)), device_id_type=MESH
            )
            peers += 1

    spans = {1: (8, 8, 0), 0: (0, 16, 8), -1: (0, 8, 24)}
    tiles = {1: (1, 1, 0), 0: (0, 2, 1), -1: (0, 1, 3)}

    def exists(dx, dy):
        x, y = gx + dx, gy + dy
        return (x >= 0) & (x < ngx) & (y >= 0) & (y < ngy)

    for n, (dx, dy) in enumerate(NEIGH):

        @pl.when(jnp.logical_not(exists(-dx, -dy)))
        def _():
            _, xn, xd = spans[dx]
            _, yn, yd = tiles[dy]
            m["ext"][xd : xd + xn, yd : yd + yn] = jnp.zeros((xn, yn, 16, 128), BF16)
            for name in ("rex", "rs1", "rs2"):
                m[name][n] = jnp.zeros(m[name].shape[1:], m[name].dtype)
            for name in ("rb", "rg2"):
                for c in range(2):
                    m[name][c, n] = jnp.zeros(m[name].shape[2:], F32)

    copy_f.wait()
    copy_p.wait()
    fcv, pcv = m["fcv"], m["pcv"]

    def own_rows(i):
        def counts(d, at, n):
            return fcv[d, pl.ds(at, n)].astype(F32) * 0.125

        f0, f1, f2 = counts(0, i, 4), counts(1, i, 4), counts(2, i, 4)
        before = jnp.where(i > 0, counts(0, jnp.maximum(i - 1, 0), 1), 0.0)
        low_x = jnp.concatenate([before, f0[:3]], axis=0)
        low_y = jnp.where(rows(f1.shape) == 0, 0.0, roll(f1, 1, 1))
        low_z = jnp.where(lanes(f2.shape) == 0, 0.0, roll(f2, 1, 2))
        src = (low_x - f0) + (low_y - f1) + (low_z - f2)
        scr = pcv[pl.ds(i, 4)].astype(F32) * 0.25
        m["scrown"][pl.ds(i, 4)] = scr
        for t in range(2):
            part = slice(8 * t, 8 * t + 8)
            m["ext"][pl.ds(i + 8, 4), t + 1] = jnp.concatenate([src[:, part], scr[:, part]], axis=1).astype(BF16)

    sweep(0, 16, 4, own_rows)

    tile_shape = (8, 128)
    sub = rows(tile_shape)
    lane = lanes(tile_shape)
    face_x = fcv[0, 15].astype(F32) * 0.125
    own_fx = [face_x[0:8], face_x[8:16]]
    own_fy = []
    for h in range(2):
        total = jnp.zeros(tile_shape, F32)
        for r in range(8):
            row = fcv[1, 8 * h + r, 15:16].astype(F32) * 0.125
            total = jnp.where(sub == r, row, total)
        own_fy.append(total)
    for t in range(2):
        m["exs"][t] = jnp.concatenate([own_fx[t], own_fy[t]], axis=0).astype(BF16)

    pl.semaphore_wait(barrier, peers)

    sent = []

    def exchange(kind, make):
        copies = []
        for n, (dx, dy) in enumerate(NEIGH):
            src, dst = make(n, dx, dy)
            copy = pltpu.make_async_remote_copy(
                src_ref=src,
                dst_ref=dst,
                send_sem=m["snd"].at[kind, n],
                recv_sem=m["rcv"].at[kind, n],
                device_id=(wrap_x(gx + dx), wrap_y(gy + dy)),
                device_id_type=MESH,
            )
            pl.when(exists(dx, dy))(copy.start)
            copies.append(copy)
        sent.append(copies)
        return copies

    def arrive(copies):
        for copy, (dx, dy) in zip(copies, NEIGH):
            pl.when(exists(-dx, -dy))(copy.wait_recv)

    def from_source(px, py):
        return NEIGH.index((-px, -py))

    def make_in(n, dx, dy):
        xs, xn, xd = spans[dx]
        ys, yn, yd = tiles[dy]
        src = m["ext"].at[pl.ds(xs + 8, xn), pl.ds(ys + 1, yn)]
        dst = m["ext"].at[pl.ds(xd, xn), pl.ds(yd, yn)]
        return src, dst

    copies_face = exchange(EX_FACE, lambda n, dx, dy: (m["exs"], m["rex"].at[n]))
    copies_in = exchange(EX_IN, make_in)

    for name in ("x0", "y0", "x1", "y1", "x2", "y2"):
        ref = m[name]
        count, width = ref.shape[:2]
        ref[0] = jnp.zeros((width, 128), F32)
        ref[count - 1] = jnp.zeros((width, 128), F32)
        ref[1 : count - 1, 0:8] = jnp.zeros((count - 2, 8, 128), F32)
        ref[1 : count - 1, width - 8 : width] = jnp.zeros((count - 2, 8, 128), F32)

    own1 = []
    for i in range(8):
        total = jnp.zeros(tile_shape, F32)
        for q in range(2):
            for j in range(2):
                total = total + m["scrown"][2 * i + q, pl.ds(j, 8, stride=2), :]
        v = zpair(total, 1) * 0.125
        m["s1own"][i] = v
        own1.append(v)
    for k in range(4):
        m["s1p"][k] = jnp.concatenate([own1[2 * k], own1[2 * k + 1]], axis=0).astype(BF16)
    copies_s1 = exchange(EX_S1, lambda n, dx, dy: (m["s1p"], m["rs1"].at[n]))

    own3 = []
    for xi in range(2):
        pair = jnp.zeros((4, 128), F32)
        for q in range(2):
            quad = jnp.zeros((4, 128), F32)
            for h in range(2):
                for j in range(2):
                    quad = quad + m["s1own"][4 * xi + 2 * q + h, pl.ds(j, 4, stride=2), :]
            pair = pair + zpair(quad, 2) * 0.125
        pair = zpair(pair, 4) * 0.125
        own3 += [pair[0:1] + pair[1:2], pair[2:3] + pair[3:4]]
    m["tile"][2] = jnp.concatenate(own3, axis=0)

    def gather_one(c):
        for o in range(1, ngy):
            pltpu.make_async_remote_copy(
                src_ref=m["tile"].at[c],
                dst_ref=m["p1"].at[c, o - 1],
                send_sem=m["ags"].at[c, 0],
                recv_sem=m["ags"].at[c, 1],
                device_id=(gx, wrap_y(gy + o)),
                device_id_type=MESH,
            ).start()

    def wait_bytes(ref, sem):
        pltpu.make_async_copy(ref, ref, sem).wait()

    def gather_two(c):
        wait_bytes(m["p1"].at[c, pl.ds(0, ngy - 1)], m["ags"].at[c, 1])
        slot = lanes((4, 128)) & 7
        total = jnp.where(slot == gy, m["tile"][c], 0.0)
        for o in range(1, ngy):
            total = jnp.where(slot == wrap_y(gy - o), m["p1"][c, o - 1], total)
        m["agb"][c, gx] = total

        for o in sorted(range(1, ngx), key=lambda o: -(min(o % 8, 8 - o % 8) + min(o // 8, 4 - o // 8))):
            pltpu.make_async_remote_copy(
                src_ref=m["agb"].at[c, gx],
                dst_ref=m["agb"].at[c, gx],
                send_sem=m["ags"].at[c, 2],
                recv_sem=m["ags"].at[c, 3],
                device_id=(wrap_x(gx + o), gy),
                device_id_type=MESH,
            ).start()

    def gather_done(c):
        wait_bytes(m["agb"].at[c, pl.ds(0, ngx - 1)], m["ags"].at[c, 3])
        return jnp.concatenate([m["agb"][c, 0:half], m["agb"][c, half:ngx]], axis=1)

    gather_one(2)

    arrive(copies_face)
    gate_x = jnp.where(gx > 0, 1.0, 0.0)
    gate_y = jnp.where(gy > 0, 1.0, 0.0)

    def face(px, py, t):
        return m["rex"][from_source(px, py), t].astype(F32)

    m["fy1"][0:8] = face(-1, -1, 1)[8:16] * gate_y
    m["fy1"][8:16] = face(0, -1, 0)[8:16] * gate_y
    m["fy1"][16:24] = face(0, -1, 1)[8:16] * gate_y
    m["fy1"][24:32] = face(1, -1, 0)[8:16] * gate_y
    m["fy2"][0:8] = face(-1, 0, 1)[8:16]
    m["fy2"][8:16] = own_fy[0]
    m["fy2"][16:24] = own_fy[1]
    m["fy2"][24:32] = face(1, 0, 0)[8:16]
    arrive(copies_in)

    def inside(shape, i, level, off):
        x = lax.broadcasted_iota(jnp.int32, shape, 0) + (i - off + gx * (16 >> level))
        y = rows(shape) + (gy * (16 >> level) - off)
        return (x >= 0) & (x < (nx0 >> level)) & (y >= 0) & (y < (ny0 >> level))

    def weight(dg, i, level, off):
        return jnp.where(inside(dg.shape, i, level, off), C1 / dg, 0.0)

    def unpack_in(i):
        n = 4
        for t in range(4):
            part = slice(8 * t, 8 * t + 8)
            pair = m["ext"][pl.ds(i, n), t].astype(F32)
            src = pair[:, 0:8]
            if t % 2 == 1:
                edge = m["fy1" if t == 1 else "fy2"]
                src = jnp.concatenate(
                    [(src[q] + jnp.where(sub == 0, edge[pl.ds(i + q, 1)], 0.0))[None] for q in range(n)], axis=0
                )
            dg = 6.0 + pair[:, 8:16]
            x = lax.broadcasted_iota(jnp.int32, dg.shape, 0) + (i - 8 + gx * 16)
            y = rows(dg.shape) + (gy * 16 - 8 + 8 * t)
            mask = (x >= 0) & (x < nx0) & (y >= 0) & (y < ny0)
            w = jnp.where(mask, C1 / dg, 0.0)
            m["g0"][pl.ds(i, n), part] = src
            m["dg0"][pl.ds(i, n), part] = dg
            m["w0"][pl.ds(i, n), part] = w
            m["x0"][pl.ds(i + 1, n), 8 * t + 8 : 8 * t + 16] = src * w

    sweep(0, 32, 4, unpack_in)
    for t, (py, k) in enumerate(((-1, 1), (0, 0), (0, 1), (1, 0))):
        part = slice(8 * t, 8 * t + 8)
        upper = own_fx[k] if py == 0 else face(0, py, k)[0:8]
        for at, extra in ((8, face(-1, py, k)[0:8] * gate_x), (24, upper)):
            total = m["g0"][at, part] + extra
            m["g0"][at, part] = total
            m["x0"][at + 1, 8 * t + 8 : 8 * t + 16] = total * m["w0"][at, part]

    lv0 = Level(m["x0"], m["y0"], m["g0"], m["w0"], m["dg0"], 0)
    lv1 = Level(m["x1"], m["y1"], m["g1"], m["w1"], m["dg1"], 1)
    lv2 = Level(m["x2"], m["y2"], m["g2"], m["w2"], m["dg2"], 2)

    def make_weights(level, scr, step, count, off):
        def body(i):
            dg = 6.0 + scr[pl.ds(i, step)] * float(4**level.depth)
            level.dg[pl.ds(i, step)] = dg
            level.w[pl.ds(i, step)] = weight(dg, i, level.depth, off)

        sweep(0, count, step, body)

    odd = (lane & 1) == 1
    copies_b = [None, None]
    copies_g = [None, None]

    def send_b(c):
        def store(i, n, r):
            m["r0"][pl.ds(i - 8, n)] = r[:, 8:24]

        lv0.residual(8, 24, 8, store)
        fine = []
        for i in range(8):
            total = jnp.zeros(tile_shape, F32)
            for q in range(2):
                for j in range(2):
                    total = total + m["r0"][2 * i + q, pl.ds(j, 8, stride=2), :]
            v = zpair(total, 1) * 0.5
            m["g1"][8 + i, 8:16] = v
            fine.append(v)
        for k in range(4):
            m["pk"][c, k] = jnp.where(odd, fine[2 * k + 1], fine[2 * k])

        def make(n, dx, dy):
            count = 4 if dx == 0 or (c == 0 and dy == 0) else 3
            part = pl.ds(4 - count if dx == 1 else 0, count)
            return m["pk"].at[c, part], m["rb"].at[c, n, part]

        copies_b[c] = exchange(EX_B + c, make)

    def take_b(c):
        arrive(copies_b[c])
        for n, (dx, dy) in enumerate(NEIGH):
            base = 8 - 8 * dx
            part = slice(8 - 8 * dy, 16 - 8 * dy)
            ks = range(4) if dx == 0 or (c == 0 and dy == 0) else (range(1, 4) if dx == 1 else range(3))
            for k in ks:
                v = m["rb"][c, n, k]
                m["g1"][base + 2 * k, part] = jnp.where(odd, roll(v, 1, 1), v)
                m["g1"][base + 2 * k + 1, part] = jnp.where(odd, v, roll(v, 127, 1))

    def setup_level1():
        arrive(copies_s1)
        for i in range(8):
            m["s1"][8 + i, 8:16] = m["s1own"][i]
        for n, (dx, dy) in enumerate(NEIGH):
            base = 8 - 8 * dx
            part = slice(8 - 8 * dy, 16 - 8 * dy)
            for k in range(4):
                v = m["rs1"][n, k].astype(F32)
                m["s1"][base + 2 * k, part] = v[0:8]
                m["s1"][base + 2 * k + 1, part] = v[8:16]
        make_weights(lv1, m["s1"], 8, 24, 8)
        for i in range(8):
            total = jnp.zeros(tile_shape, F32)
            for q in range(2):
                for j in range(2):
                    total = total + m["s1"][4 + 2 * i + q, pl.ds(4 + j, 8, stride=2), :]
            m["s2t"][i] = zpair(total, 2) * 0.125
        m["w2t"][...] = weight(6.0 + m["s2t"][...] * 16.0, 0, 2, 2)

    def exchange_tile(kind, src, dst):
        def make(n, dx, dy):
            part = {1: pl.ds(0, 4), 0: pl.ds(0, 8), -1: pl.ds(4, 4)}[dx]
            return src.at[part], dst.at[n, part]

        return exchange(kind, make)

    def assemble(own, got, out):
        for i in range(16):
            px = -1 if i < 4 else (0 if i < 12 else 1)
            r = i - 4 * px - 4
            for py, part in ((-1, slice(0, 8)), (1, slice(8, 16)), (0, slice(4, 12))):
                out[i, part] = own[r] if (px, py) == (0, 0) else got[from_source(px, py), r]

    def pre_level1(c):
        lv1.first_zero(0, 24, 8)
        lv1.second_zero(0, 24, 8)

        def store(i, n, r):
            m["r1"][pl.ds(i - 4, n)] = r

        lv1.residual(4, 20, 8, store)
        small = []
        for i in range(8):
            total = jnp.zeros(tile_shape, F32)
            for q in range(2):
                for j in range(2):
                    total = total + m["r1"][2 * i + q, pl.ds(4 + j, 8, stride=2), :]
            small.append((zpair(total, 2) * 0.5)[None])
        g = jnp.concatenate(small, axis=0)
        m["g2t"][c] = g
        dg = 6.0 + m["s2t"][...] * 16.0
        w = m["w2t"][...]
        zero = jnp.zeros((1, 8, 128), F32)

        def around(v):
            up = jnp.concatenate([v[1:], zero], axis=0)
            dn = jnp.concatenate([zero, v[:-1]], axis=0)
            return g + side_sum(v, up, dn, 4)

        v = g * w
        v = K1 * v + K2 * (around(v) * w)
        r = around(v) - dg * v
        parts = []
        for xi in range(2):
            t = r[2 + 2 * xi] + r[3 + 2 * xi]
            t = zpair(t + roll(t, 7, 0), 4) * 0.5
            parts += [t[2:3], t[4:5]]
        m["tile"][c] = jnp.concatenate(parts, axis=0)

    def dot(a, b):
        t = a * b
        while t.shape[0] > 1:
            h = t.shape[0] // 2
            t = t[:h] + t[h:]
        t = jnp.sum(t[0], axis=0, keepdims=True)
        return jnp.sum(t, axis=1, keepdims=True)[None]

    full = (half, 8, 128)
    lane3 = lanes(full)
    sub3 = rows(full)
    slot3 = lane3 & 7
    even_y = (sub3 & 1) == 0
    even_x = (sub3 & 2) == 0
    low_y = even_y & (slot3 > 0)
    high_y = jnp.logical_not(even_y) & (slot3 < ngy - 1)

    def image3(f, dg):
        swap = jnp.where(even_y, roll(f, 7, 1), roll(f, 1, 1))
        total = swap + jnp.where(low_y, roll(swap, 1, 2), jnp.where(high_y, roll(swap, 127, 2), 0.0))
        left = roll(f, 6, 1)
        right = roll(f, 2, 1)
        after = jnp.where(sub < 4, left[0], 0.0)[None]
        ahead = jnp.where(sub >= 4, right[half - 1], 0.0)[None]
        nxt = jnp.concatenate([right[1:], after], axis=0)
        prv = jnp.concatenate([ahead, left[:-1]], axis=0)
        total = total + jnp.where(even_x, left + prv, right + nxt)
        total = total + jnp.where(lane3 < 8, 0.0, roll(f, 8, 2))
        total = total + jnp.where(lane3 >= 120, 0.0, roll(f, 120, 2))
        q = dg * f - total
        return q if ngy == 8 else jnp.where(slot3 < ngy, q, 0.0)

    def coarse(r):
        dg = m["dg3"][...]
        x = p = q = rr_old = curve = None
        for it in range(COARSE_ITERS):
            image = image3(r, dg)
            rr = dot(r, r)
            rar = dot(r, image)
            if it == 0:
                p, q, curve = r, image, rar
            else:
                beta = rr / rr_old
                curve = rar - beta * beta * curve
                p = r + beta * p
                q = image + beta * q
            alpha = rr / curve
            x = alpha * p if it == 0 else x + alpha * p
            if it + 1 < COARSE_ITERS:
                r = r - alpha * q
            rr_old = rr
        m["e3"][...] = x

    step_y = (sub + 1) >> 1
    pick = (lane & 7) == step_y

    def post_level2():
        for k in range(8):
            a, xi = (k - 3) >> 1, (k - 3) & 1
            at = wrap_x(gx + a)
            b = at // half
            v = at - b * half
            low = m["e3"][v, pl.ds(4 * b + 2 * xi, 1)]
            high = m["e3"][v, pl.ds(4 * b + 2 * xi + 1, 1)]
            t = jnp.where((sub & 1) == 1, low, high)
            t = roll(t, lax.rem(130 - gy, 128), 1)
            t = jnp.where(pick, t, 0.0)
            for width in (4, 2, 1):
                t = jnp.where((step_y & width) != 0, roll(t, 128 - width, 1), t)
            for width in (1, 2, 4):
                t = t + roll(t, width, 1)
            m["pe2"][k, pl.ds(0, 8, stride=2), :] = t
            m["pe2"][k, pl.ds(1, 8, stride=2), :] = t
        for i in range(16):
            m["y2"][i + 1, 8:24] = m["y2"][i + 1, 8:24] + jnp.where(m["w2"][i] != 0.0, m["pe2"][i // 2], 0.0)
        lv2.pass_one(1, 15, 14)
        lv2.pass_two(2, 14, 12)

    def post_level1(c):
        lo, hi = ((2, 22), (4, 20))[c]
        for i in range(lo, hi):
            e = m["y2"][i // 2 + 3, 10:22]
            for j in range(2):
                at = pl.ds(8 + j, 12, stride=2)
                m["y1"][i + 1, at, :] = m["y1"][i + 1, at, :] + e
        if c == 0:
            lv1.pass_one(3, 21, 9)
            lv1.pass_two(4, 20, 8)
        else:
            lv1.pass_one(5, 19, 7)
            lv1.pass_two(6, 18, 6)

    def post_level0(c):
        lo, hi = ((0, 32), (4, 28))[c]

        def add(k):
            for h in range(2):
                e = m["y1"][k + h + 5, 12:28]
                for q in range(2):
                    for j in range(2):
                        at = pl.ds(8 + j, 16, stride=2)
                        i = 2 * (k + h) + q + 1
                        m["y0"][i, at, :] = m["y0"][i, at, :] + e

        sweep(lo // 2, hi // 2, 2, add)
        if c == 0:
            lv0.pass_one(2, 30, 7)
            lv0.pass_two(2, 30, 7)
        else:
            lv0.pass_one(6, 26, 5)
            lv0.pass_two(7, 25, 6)

    for c in range(2):
        if c == 0:
            lv0.second_zero(0, 32, 8)
        else:
            lv0.pass_one(4, 28, 8)
            lv0.pass_two(4, 28, 8)
        send_b(c)
        if c == 0:
            gather_two(2)
            setup_level1()
            copies_s2 = exchange_tile(EX_S2, m["s2t"], m["rs2"])
        take_b(c)
        pre_level1(c)
        gather_one(c)
        copies_g[c] = exchange_tile(EX_G + c, m["g2t"].at[c], m["rg2"].at[c])
        if c == 0:
            arrive(copies_s2)
            assemble(m["s2t"], m["rs2"], m["s2"])
            make_weights(lv2, m["s2"], 8, 16, 6)
        gather_two(c)
        arrive(copies_g[c])
        assemble(m["g2t"].at[c], m["rg2"].at[c], m["g2"])
        lv2.first_zero(0, 16, 16)
        lv2.second_zero(1, 15, 14)
        if c == 0:
            m["dg3"][...] = 6.0 + gather_done(2) * 64.0
        if c == 1:
            for copies in sent:
                for copy, (dx, dy) in zip(copies, NEIGH):
                    pl.when(exists(dx, dy))(copy.wait_send)
            for k in range(3):
                wait_bytes(m["p1"].at[k, pl.ds(0, ngy - 1)], m["ags"].at[k, 0])
                wait_bytes(m["agb"].at[k, pl.ds(0, ngx - 1)], m["ags"].at[k, 2])
        coarse(gather_done(c))
        post_level2()
        post_level1(c)
        post_level0(c)

    def store(i, n, r):
        res_ref[pl.ds(i - 8, n)] = r[:, 8:24]
        sol_ref[pl.ds(i - 8, n)] = m["y0"][pl.ds(i + 1, n), 16:32]

    lv0.residual(8, 24, 8, store)


def solution(mesh):
    ngx, ngy = mesh.shape["gx"], mesh.shape["gy"]
    items = scratch_list(ngx)
    names = tuple(name for name, _ in items)

    def per_device(point_counts, face_counts):
        shape = jax.ShapeDtypeStruct(point_counts.shape, F32)
        return pl.pallas_call(
            functools.partial(kernel, ngx, ngy, names),
            out_shape=(shape, shape),
            in_specs=[pl.BlockSpec(memory_space=pltpu.HBM)] * 2,
            out_specs=(pl.BlockSpec(memory_space=pltpu.VMEM),) * 2,
            scratch_shapes=[spec for _, spec in items],
            compiler_params=pltpu.CompilerParams(
                collective_id=0, has_side_effects=True, vmem_limit_bytes=54880 * 1024
            ),
            name="poisson",
        )(point_counts, face_counts)

    return jax.shard_map(
        per_device,
        mesh=mesh,
        in_specs=(P("gx", "gy", None), P(None, "gx", "gy", None)),
        out_specs=(P("gx", "gy", None), P("gx", "gy", None)),
        check_vma=False,
    )
```

```python
import functools

import jax
import jax.numpy as jnp
from jax import lax
from jax.experimental import pallas as pl
from jax.experimental.pallas import tpu as pltpu
from jax.sharding import PartitionSpec as P


MESH = pl.DeviceIdType.MESH
F32 = jnp.float32
BF16 = jnp.bfloat16
NEIGH = ((-1, -1), (-1, 1), (1, -1), (1, 1), (-1, 0), (1, 0), (0, -1), (0, 1))

CENTRE = 0.5 * (2.0 + 0.3)
RADIUS = 0.5 * (2.0 - 0.3)
RATIO = CENTRE / RADIUS
MOM = 1.0 / RATIO
MOM2 = 1.0 / (2.0 * RATIO - MOM)
C1 = 1.0 / CENTRE
CA = MOM2 * MOM
CB = 2.0 * MOM2 / RADIUS
K0 = 1.0 - C1
K1 = 1.0 + CA - CB
K2 = CB / C1
COARSE_ITERS = 6


def lanes(shape):
    return lax.broadcasted_iota(jnp.int32, shape, len(shape) - 1)


def rows(shape):
    return lax.broadcasted_iota(jnp.int32, shape, len(shape) - 2)


def roll(v, shift, axis):
    return pltpu.roll(v, shift, axis)


def zpair(v, width):
    axis = v.ndim - 1
    low = (lanes(v.shape) & width) == 0
    return v + jnp.where(low, roll(v, 128 - width, axis), roll(v, width, axis))


def side_sum(c, up, dn, shift):
    ax = c.ndim - 2
    count = c.shape[ax]
    lane = lanes(c.shape)
    total = up + dn
    total = total + (roll(c, 1, ax) + roll(c, count - 1, ax))
    low = jnp.where(lane < shift, 0.0, roll(c, shift, ax + 1))
    high = jnp.where(lane >= 128 - shift, 0.0, roll(c, 128 - shift, ax + 1))
    return total + (low + high)


def sweep(lo, hi, step, body):
    def one(k, carry):
        body(lo + k * step)
        return carry

    lax.fori_loop(0, (hi - lo) // step, one, 0, unroll=True)


def far_first(ngx):
    return sorted(range(1, ngx), key=lambda o: -(min(o % 8, 8 - o % 8) + min(o // 8, 4 - o // 8)))


class Level:
    def __init__(self, x, y, g, w, dg, depth):
        self.x, self.y, self.g, self.w, self.dg = x, y, g, w, dg
        self.depth = depth
        self.shift = 2**depth
        self.count = g.shape[1]
        self.mid = slice(8, 8 + self.count)

    def around(self, src, i, n):
        c = src[pl.ds(i + 1, n), self.mid]
        lane = lanes(c.shape)
        total = src[pl.ds(i + 2, n), self.mid] + src[pl.ds(i, n), self.mid]
        total = total + (src[pl.ds(i + 1, n), 7 : 7 + self.count] + src[pl.ds(i + 1, n), 9 : 9 + self.count])
        low = jnp.where(lane < self.shift, 0.0, roll(c, self.shift, 2))
        high = jnp.where(lane >= 128 - self.shift, 0.0, roll(c, 128 - self.shift, 2))
        return c, (total + self.g[pl.ds(i, n)]) + (low + high)

    def first_zero(self, lo, hi, n):
        def body(i):
            self.x[pl.ds(i + 1, n), self.mid] = self.g[pl.ds(i, n)] * self.w[pl.ds(i, n)]

        sweep(lo, hi, n, body)

    def second_zero(self, lo, hi, n):
        def body(i):
            c, t = self.around(self.x, i, n)
            self.y[pl.ds(i + 1, n), self.mid] = K1 * c + K2 * (t * self.w[pl.ds(i, n)])

        sweep(lo, hi, n, body)

    def pass_one(self, lo, hi, n):
        def body(i):
            c, t = self.around(self.y, i, n)
            self.x[pl.ds(i + 1, n), self.mid] = K0 * c + t * self.w[pl.ds(i, n)]

        sweep(lo, hi, n, body)

    def pass_two(self, lo, hi, n):
        def body(i):
            c, t = self.around(self.x, i, n)
            old = self.y[pl.ds(i + 1, n), self.mid]
            self.y[pl.ds(i + 1, n), self.mid] = (K1 * c - CA * old) + K2 * (t * self.w[pl.ds(i, n)])

        sweep(lo, hi, n, body)

    def residual(self, lo, hi, n, store):
        def body(i):
            c, t = self.around(self.y, i, n)
            store(i, n, t - self.dg[pl.ds(i, n)] * c)

        sweep(lo, hi, n, body)


def scratch_list(ngx):
    v = pltpu.VMEM
    return (
        ("fcv", v((3, 16, 16, 128), jnp.int32)),
        ("pcv", v((16, 16, 128), jnp.int32)),
        ("ext", v((32, 4, 16, 128), BF16)),
        ("exs", v((2, 16, 128), BF16)),
        ("rex", v((8, 2, 16, 128), BF16)),
        ("s1p", v((4, 16, 128), BF16)),
        ("rs1", v((8, 4, 16, 128), BF16)),
        ("scrown", v((16, 16, 128), F32)),
        ("s1own", v((8, 8, 128), F32)),
        ("fy1", v((32, 128), F32)),
        ("fy2", v((32, 128), F32)),
        ("x0", v((34, 48, 128), F32)),
        ("y0", v((34, 48, 128), F32)),
        ("g0", v((32, 32, 128), F32)),
        ("w0", v((32, 32, 128), F32)),
        ("dg0", v((32, 32, 128), F32)),
        ("r0", v((16, 16, 128), F32)),
        ("pk", v((2, 4, 8, 128), F32)),
        ("rb", v((2, 8, 4, 8, 128), F32)),
        ("x1", v((26, 40, 128), F32)),
        ("y1", v((26, 40, 128), F32)),
        ("g1", v((24, 24, 128), F32)),
        ("s1", v((24, 24, 128), F32)),
        ("w1", v((24, 24, 128), F32)),
        ("dg1", v((24, 24, 128), F32)),
        ("r1", v((16, 24, 128), F32)),
        ("s2t", v((8, 8, 128), F32)),
        ("w2t", v((8, 8, 128), F32)),
        ("rs2", v((8, 8, 8, 128), F32)),
        ("g2t", v((2, 8, 8, 128), F32)),
        ("rg2", v((2, 8, 8, 8, 128), F32)),
        ("x2", v((18, 32, 128), F32)),
        ("y2", v((18, 32, 128), F32)),
        ("g2", v((16, 16, 128), F32)),
        ("s2", v((16, 16, 128), F32)),
        ("w2", v((16, 16, 128), F32)),
        ("dg2", v((16, 16, 128), F32)),
        ("pe2", v((8, 16, 128), F32)),
        ("tile", v((3, 4, 128), F32)),
        ("p1", v((3, 7, 4, 128), F32)),
        ("agb", v((3, ngx, 4, 128), F32)),
        ("dg3", v((ngx // 2, 8, 128), F32)),
        ("e3", v((ngx // 2, 8, 128), F32)),
        ("snd", pltpu.SemaphoreType.DMA((8, 8))),
        ("rcv", pltpu.SemaphoreType.DMA((8, 8))),
        ("ags", pltpu.SemaphoreType.DMA((3, 4))),
        ("loc", pltpu.SemaphoreType.DMA((2,))),
    )


EX_IN, EX_FACE, EX_S1, EX_S2, EX_B, EX_G = 0, 1, 2, 3, 4, 6


def kernel(ngx, ngy, names, pc_hbm, fc_hbm, sol_ref, res_ref, *scratch):
    m = dict(zip(names, scratch))
    gx = lax.axis_index("gx")
    gy = lax.axis_index("gy")
    half = ngx // 2
    nx0, ny0 = 16 * ngx, 16 * ngy

    def wrap_x(v):
        return lax.rem(v + ngx, ngx)

    def wrap_y(v):
        return lax.rem(v + ngy, ngy)

    copy_p = pltpu.make_async_copy(pc_hbm, m["pcv"], m["loc"].at[0])
    copy_f = pltpu.make_async_copy(fc_hbm, m["fcv"], m["loc"].at[1])
    copy_p.start()
    copy_f.start()

    barrier = pltpu.get_barrier_semaphore()
    met = [(o, 0) for o in far_first(ngx)]
    met += [(dx, dy) for dx, dy in NEIGH if dx != 0 and dy != 0]
    met += [(0, o) for o in range(1, ngy)]
    for dx, dy in met:
        pl.semaphore_signal(
            barrier, inc=1, device_id=(wrap_x(gx + dx), wrap_y(gy + dy)), device_id_type=MESH
        )

    spans = {1: (8, 8, 0), 0: (0, 16, 8), -1: (0, 8, 24)}
    tiles = {1: (1, 1, 0), 0: (0, 2, 1), -1: (0, 1, 3)}

    def exists(dx, dy):
        x, y = gx + dx, gy + dy
        return (x >= 0) & (x < ngx) & (y >= 0) & (y < ngy)

    copy_f.wait()
    copy_p.wait()
    fcv, pcv = m["fcv"], m["pcv"]

    def own_rows(i):
        def counts(d, at, n):
            return fcv[d, pl.ds(at, n)].astype(F32) * 0.125

        f0, f1, f2 = counts(0, i, 4), counts(1, i, 4), counts(2, i, 4)
        before = jnp.where(i > 0, counts(0, jnp.maximum(i - 1, 0), 1), 0.0)
        low_x = jnp.concatenate([before, f0[:3]], axis=0)
        low_y = jnp.where(rows(f1.shape) == 0, 0.0, roll(f1, 1, 1))
        low_z = jnp.where(lanes(f2.shape) == 0, 0.0, roll(f2, 1, 2))
        src = (low_x - f0) + (low_y - f1) + (low_z - f2)
        scr = pcv[pl.ds(i, 4)].astype(F32) * 0.25
        m["scrown"][pl.ds(i, 4)] = scr
        for t in range(2):
            part = slice(8 * t, 8 * t + 8)
            m["ext"][pl.ds(i + 8, 4), t + 1] = jnp.concatenate([src[:, part], scr[:, part]], axis=1).astype(BF16)

    sweep(0, 16, 4, own_rows)

    tile_shape = (8, 128)
    sub = rows(tile_shape)
    lane = lanes(tile_shape)
    face_x = fcv[0, 15].astype(F32) * 0.125
    own_fx = [face_x[0:8], face_x[8:16]]
    own_fy = []
    for h in range(2):
        total = jnp.zeros(tile_shape, F32)
        for r in range(8):
            row = fcv[1, 8 * h + r, 15:16].astype(F32) * 0.125
            total = jnp.where(sub == r, row, total)
        own_fy.append(total)
    for t in range(2):
        m["exs"][t] = jnp.concatenate([own_fx[t], own_fy[t]], axis=0).astype(BF16)

    pl.semaphore_wait(barrier, len(met))

    sent = []

    def exchange(kind, make):
        copies = []
        for n, (dx, dy) in enumerate(NEIGH):
            src, dst = make(n, dx, dy)
            copy = pltpu.make_async_remote_copy(
                src_ref=src,
                dst_ref=dst,
                send_sem=m["snd"].at[kind, n],
                recv_sem=m["rcv"].at[kind, n],
                device_id=(wrap_x(gx + dx), wrap_y(gy + dy)),
                device_id_type=MESH,
            )
            pl.when(exists(dx, dy))(copy.start)
            copies.append(copy)
        sent.append(copies)
        return copies

    def arrive(copies):
        for copy, (dx, dy) in zip(copies, NEIGH):
            pl.when(exists(-dx, -dy))(copy.wait_recv)

    def from_source(px, py):
        return NEIGH.index((-px, -py))

    def make_in(n, dx, dy):
        xs, xn, xd = spans[dx]
        ys, yn, yd = tiles[dy]
        src = m["ext"].at[pl.ds(xs + 8, xn), pl.ds(ys + 1, yn)]
        dst = m["ext"].at[pl.ds(xd, xn), pl.ds(yd, yn)]
        return src, dst

    def make_face(n, dx, dy):
        first, count = (0, 2) if (dx, dy) in ((1, 0), (0, 1)) else ((1, 1) if (dx, dy) == (1, 1) else (0, 1))
        part = pl.ds(first, count)
        return m["exs"].at[part], m["rex"].at[n, part]

    copies_face = exchange(EX_FACE, make_face)
    copies_in = exchange(EX_IN, make_in)

    for n, (dx, dy) in enumerate(NEIGH):

        @pl.when(jnp.logical_not(exists(-dx, -dy)))
        def _():
            _, xn, xd = spans[dx]
            _, yn, yd = tiles[dy]
            m["ext"][xd : xd + xn, yd : yd + yn] = jnp.zeros((xn, yn, 16, 128), BF16)
            for name in ("rex", "rs1", "rs2"):
                m[name][n] = jnp.zeros(m[name].shape[1:], m[name].dtype)
            for name in ("rb", "rg2"):
                for c in range(2):
                    m[name][c, n] = jnp.zeros(m[name].shape[2:], F32)

    for name in ("x0", "y0", "x1", "y1", "x2", "y2"):
        ref = m[name]
        count, width = ref.shape[:2]
        ref[0] = jnp.zeros((width, 128), F32)
        ref[count - 1] = jnp.zeros((width, 128), F32)
        ref[1 : count - 1, 0:8] = jnp.zeros((count - 2, 8, 128), F32)
        ref[1 : count - 1, width - 8 : width] = jnp.zeros((count - 2, 8, 128), F32)

    own1 = []
    for i in range(8):
        total = jnp.zeros(tile_shape, F32)
        for q in range(2):
            for j in range(2):
                total = total + m["scrown"][2 * i + q, pl.ds(j, 8, stride=2), :]
        v = zpair(total, 1) * 0.125
        m["s1own"][i] = v
        own1.append(v)
    for k in range(4):
        m["s1p"][k] = jnp.concatenate([own1[2 * k], own1[2 * k + 1]], axis=0).astype(BF16)
    copies_s1 = exchange(EX_S1, lambda n, dx, dy: (m["s1p"], m["rs1"].at[n]))

    own3 = []
    for xi in range(2):
        pair = jnp.zeros((4, 128), F32)
        for q in range(2):
            quad = jnp.zeros((4, 128), F32)
            for h in range(2):
                for j in range(2):
                    quad = quad + m["s1own"][4 * xi + 2 * q + h, pl.ds(j, 4, stride=2), :]
            pair = pair + zpair(quad, 2) * 0.125
        pair = zpair(pair, 4) * 0.125
        own3 += [pair[0:1] + pair[1:2], pair[2:3] + pair[3:4]]
    m["tile"][2] = jnp.concatenate(own3, axis=0)

    def gather_one(c):
        for o in range(1, ngy):
            pltpu.make_async_remote_copy(
                src_ref=m["tile"].at[c],
                dst_ref=m["p1"].at[c, o - 1],
                send_sem=m["ags"].at[c, 0],
                recv_sem=m["ags"].at[c, 1],
                device_id=(gx, wrap_y(gy + o)),
                device_id_type=MESH,
            ).start()

    def wait_bytes(ref, sem):
        pltpu.make_async_copy(ref, ref, sem).wait()

    def gather_two(c):
        wait_bytes(m["p1"].at[c, pl.ds(0, ngy - 1)], m["ags"].at[c, 1])
        slot = lanes((4, 128)) & 7
        total = jnp.where(slot == gy, m["tile"][c], 0.0)
        for o in range(1, ngy):
            total = jnp.where(slot == wrap_y(gy - o), m["p1"][c, o - 1], total)
        m["agb"][c, gx] = total

        for o in far_first(ngx):
            pltpu.make_async_remote_copy(
                src_ref=m["agb"].at[c, gx],
                dst_ref=m["agb"].at[c, gx],
                send_sem=m["ags"].at[c, 2],
                recv_sem=m["ags"].at[c, 3],
                device_id=(wrap_x(gx + o), gy),
                device_id_type=MESH,
            ).start()

    def gather_done(c):
        wait_bytes(m["agb"].at[c, pl.ds(0, ngx - 1)], m["ags"].at[c, 3])
        return jnp.concatenate([m["agb"][c, 0:half], m["agb"][c, half:ngx]], axis=1)

    gather_one(2)

    arrive(copies_face)
    gate_x = jnp.where(gx > 0, 1.0, 0.0)
    gate_y = jnp.where(gy > 0, 1.0, 0.0)

    def face(px, py, t):
        return m["rex"][from_source(px, py), t].astype(F32)

    m["fy1"][0:8] = face(-1, -1, 1)[8:16] * gate_y
    m["fy1"][8:16] = face(0, -1, 0)[8:16] * gate_y
    m["fy1"][16:24] = face(0, -1, 1)[8:16] * gate_y
    m["fy1"][24:32] = face(1, -1, 0)[8:16] * gate_y
    m["fy2"][0:8] = face(-1, 0, 1)[8:16]
    m["fy2"][8:16] = own_fy[0]
    m["fy2"][16:24] = own_fy[1]
    m["fy2"][24:32] = face(1, 0, 0)[8:16]
    arrive(copies_in)

    def inside(shape, i, level, off):
        x = lax.broadcasted_iota(jnp.int32, shape, 0) + (i - off + gx * (16 >> level))
        y = rows(shape) + (gy * (16 >> level) - off)
        return (x >= 0) & (x < (nx0 >> level)) & (y >= 0) & (y < (ny0 >> level))

    def weight(dg, i, level, off):
        return jnp.where(inside(dg.shape, i, level, off), C1 / dg, 0.0)

    def unpack_in(i):
        n = 4
        for t in range(4):
            part = slice(8 * t, 8 * t + 8)
            pair = m["ext"][pl.ds(i, n), t].astype(F32)
            src = pair[:, 0:8]
            if t % 2 == 1:
                edge = m["fy1" if t == 1 else "fy2"]
                src = jnp.concatenate(
                    [(src[q] + jnp.where(sub == 0, edge[pl.ds(i + q, 1)], 0.0))[None] for q in range(n)], axis=0
                )
            dg = 6.0 + pair[:, 8:16]
            x = lax.broadcasted_iota(jnp.int32, dg.shape, 0) + (i - 8 + gx * 16)
            y = rows(dg.shape) + (gy * 16 - 8 + 8 * t)
            mask = (x >= 0) & (x < nx0) & (y >= 0) & (y < ny0)
            w = jnp.where(mask, C1 / dg, 0.0)
            m["g0"][pl.ds(i, n), part] = src
            m["dg0"][pl.ds(i, n), part] = dg
            m["w0"][pl.ds(i, n), part] = w
            m["x0"][pl.ds(i + 1, n), 8 * t + 8 : 8 * t + 16] = src * w

    sweep(0, 32, 4, unpack_in)
    for t, (py, k) in enumerate(((-1, 1), (0, 0), (0, 1), (1, 0))):
        part = slice(8 * t, 8 * t + 8)
        upper = own_fx[k] if py == 0 else face(0, py, k)[0:8]
        for at, extra in ((8, face(-1, py, k)[0:8] * gate_x), (24, upper)):
            total = m["g0"][at, part] + extra
            m["g0"][at, part] = total
            m["x0"][at + 1, 8 * t + 8 : 8 * t + 16] = total * m["w0"][at, part]

    lv0 = Level(m["x0"], m["y0"], m["g0"], m["w0"], m["dg0"], 0)
    lv1 = Level(m["x1"], m["y1"], m["g1"], m["w1"], m["dg1"], 1)
    lv2 = Level(m["x2"], m["y2"], m["g2"], m["w2"], m["dg2"], 2)

    def make_weights(level, scr, step, count, off):
        def body(i):
            dg = 6.0 + scr[pl.ds(i, step)] * float(4**level.depth)
            level.dg[pl.ds(i, step)] = dg
            level.w[pl.ds(i, step)] = weight(dg, i, level.depth, off)

        sweep(0, count, step, body)

    odd = (lane & 1) == 1
    copies_b = [None, None]
    copies_g = [None, None]

    def send_b(c):
        def store(i, n, r):
            m["r0"][pl.ds(i - 8, n)] = r[:, 8:24]

        lv0.residual(8, 24, 8, store)
        fine = []
        for i in range(8):
            total = jnp.zeros(tile_shape, F32)
            for q in range(2):
                for j in range(2):
                    total = total + m["r0"][2 * i + q, pl.ds(j, 8, stride=2), :]
            v = zpair(total, 1) * 0.5
            m["g1"][8 + i, 8:16] = v
            fine.append(v)
        for k in range(4):
            m["pk"][c, k] = jnp.where(odd, fine[2 * k + 1], fine[2 * k])

        def make(n, dx, dy):
            count = 4 if dx == 0 or (c == 0 and dy == 0) else 3
            part = pl.ds(4 - count if dx == 1 else 0, count)
            return m["pk"].at[c, part], m["rb"].at[c, n, part]

        copies_b[c] = exchange(EX_B + c, make)

    def take_b(c):
        arrive(copies_b[c])
        for n, (dx, dy) in enumerate(NEIGH):
            base = 8 - 8 * dx
            part = slice(8 - 8 * dy, 16 - 8 * dy)
            ks = range(4) if dx == 0 or (c == 0 and dy == 0) else (range(1, 4) if dx == 1 else range(3))
            for k in ks:
                v = m["rb"][c, n, k]
                m["g1"][base + 2 * k, part] = jnp.where(odd, roll(v, 1, 1), v)
                m["g1"][base + 2 * k + 1, part] = jnp.where(odd, v, roll(v, 127, 1))

    def setup_level1():
        arrive(copies_s1)
        for i in range(8):
            m["s1"][8 + i, 8:16] = m["s1own"][i]
        for n, (dx, dy) in enumerate(NEIGH):
            base = 8 - 8 * dx
            part = slice(8 - 8 * dy, 16 - 8 * dy)
            for k in range(4):
                v = m["rs1"][n, k].astype(F32)
                m["s1"][base + 2 * k, part] = v[0:8]
                m["s1"][base + 2 * k + 1, part] = v[8:16]
        make_weights(lv1, m["s1"], 8, 24, 8)
        for i in range(8):
            total = jnp.zeros(tile_shape, F32)
            for q in range(2):
                for j in range(2):
                    total = total + m["s1"][4 + 2 * i + q, pl.ds(4 + j, 8, stride=2), :]
            m["s2t"][i] = zpair(total, 2) * 0.125
        m["w2t"][...] = weight(6.0 + m["s2t"][...] * 16.0, 0, 2, 2)

    def exchange_tile(kind, src, dst):
        def make(n, dx, dy):
            part = {1: pl.ds(0, 4), 0: pl.ds(0, 8), -1: pl.ds(4, 4)}[dx]
            return src.at[part], dst.at[n, part]

        return exchange(kind, make)

    def assemble(own, got, out):
        for i in range(16):
            px = -1 if i < 4 else (0 if i < 12 else 1)
            r = i - 4 * px - 4
            for py, part in ((-1, slice(0, 8)), (1, slice(8, 16)), (0, slice(4, 12))):
                out[i, part] = own[r] if (px, py) == (0, 0) else got[from_source(px, py), r]

    def pre_level1(c):
        lv1.first_zero(0, 24, 8)
        lv1.second_zero(0, 24, 8)

        def store(i, n, r):
            m["r1"][pl.ds(i - 4, n)] = r

        lv1.residual(4, 20, 8, store)
        small = []
        for i in range(8):
            total = jnp.zeros(tile_shape, F32)
            for q in range(2):
                for j in range(2):
                    total = total + m["r1"][2 * i + q, pl.ds(4 + j, 8, stride=2), :]
            small.append((zpair(total, 2) * 0.5)[None])
        g = jnp.concatenate(small, axis=0)
        m["g2t"][c] = g
        dg = 6.0 + m["s2t"][...] * 16.0
        w = m["w2t"][...]
        zero = jnp.zeros((1, 8, 128), F32)

        def around(v):
            up = jnp.concatenate([v[1:], zero], axis=0)
            dn = jnp.concatenate([zero, v[:-1]], axis=0)
            return g + side_sum(v, up, dn, 4)

        v = g * w
        v = K1 * v + K2 * (around(v) * w)
        r = around(v) - dg * v
        parts = []
        for xi in range(2):
            t = r[2 + 2 * xi] + r[3 + 2 * xi]
            t = zpair(t + roll(t, 7, 0), 4) * 0.5
            parts += [t[2:3], t[4:5]]
        m["tile"][c] = jnp.concatenate(parts, axis=0)

    def dot(a, b):
        t = a * b
        while t.shape[0] > 1:
            h = t.shape[0] // 2
            t = t[:h] + t[h:]
        t = jnp.sum(t[0], axis=0, keepdims=True)
        return jnp.sum(t, axis=1, keepdims=True)[None]

    full = (half, 8, 128)
    lane3 = lanes(full)
    sub3 = rows(full)
    slot3 = lane3 & 7
    even_y = (sub3 & 1) == 0
    even_x = (sub3 & 2) == 0
    low_y = even_y & (slot3 > 0)
    high_y = jnp.logical_not(even_y) & (slot3 < ngy - 1)

    def image3(f, dg):
        swap = jnp.where(even_y, roll(f, 7, 1), roll(f, 1, 1))
        total = swap + jnp.where(low_y, roll(swap, 1, 2), jnp.where(high_y, roll(swap, 127, 2), 0.0))
        left = roll(f, 6, 1)
        right = roll(f, 2, 1)
        after = jnp.where(sub < 4, left[0], 0.0)[None]
        ahead = jnp.where(sub >= 4, right[half - 1], 0.0)[None]
        nxt = jnp.concatenate([right[1:], after], axis=0)
        prv = jnp.concatenate([ahead, left[:-1]], axis=0)
        total = total + jnp.where(even_x, left + prv, right + nxt)
        total = total + jnp.where(lane3 < 8, 0.0, roll(f, 8, 2))
        total = total + jnp.where(lane3 >= 120, 0.0, roll(f, 120, 2))
        q = dg * f - total
        return q if ngy == 8 else jnp.where(slot3 < ngy, q, 0.0)

    def coarse(r):
        dg = m["dg3"][...]
        x = p = q = rr_old = curve = None
        for it in range(COARSE_ITERS):
            image = image3(r, dg)
            rr = dot(r, r)
            rar = dot(r, image)
            if it == 0:
                p, q, curve = r, image, rar
            else:
                beta = rr / rr_old
                curve = rar - beta * beta * curve
                p = r + beta * p
                q = image + beta * q
            alpha = rr / curve
            x = alpha * p if it == 0 else x + alpha * p
            if it + 1 < COARSE_ITERS:
                r = r - alpha * q
            rr_old = rr
        m["e3"][...] = x

    pick = (lane - (lane & 7)) + jnp.clip(gy - 2 + ((sub + 1) >> 1), 0, ngy - 1)

    def post_level2():
        for k in range(8):
            a, xi = (k - 3) >> 1, (k - 3) & 1
            at = wrap_x(gx + a)
            b = at // half
            v = at - b * half
            low = m["e3"][v, pl.ds(4 * b + 2 * xi, 1)]
            high = m["e3"][v, pl.ds(4 * b + 2 * xi + 1, 1)]
            t = jnp.where((sub & 1) == 1, low, high)
            t = jnp.take_along_axis(t, pick, axis=1, mode="promise_in_bounds")
            m["pe2"][k, pl.ds(0, 8, stride=2), :] = t
            m["pe2"][k, pl.ds(1, 8, stride=2), :] = t
        for i in range(16):
            m["y2"][i + 1, 8:24] = m["y2"][i + 1, 8:24] + jnp.where(m["w2"][i] != 0.0, m["pe2"][i // 2], 0.0)
        lv2.pass_one(1, 15, 14)
        lv2.pass_two(2, 14, 12)

    def post_level1(c):
        lo, hi = ((2, 22), (4, 20))[c]
        for i in range(lo, hi):
            e = m["y2"][i // 2 + 3, 10:22]
            for j in range(2):
                at = pl.ds(8 + j, 12, stride=2)
                m["y1"][i + 1, at, :] = m["y1"][i + 1, at, :] + e
        if c == 0:
            lv1.pass_one(3, 21, 9)
            lv1.pass_two(4, 20, 8)
        else:
            lv1.pass_one(5, 19, 7)
            lv1.pass_two(6, 18, 6)

    def post_level0(c):
        lo, hi = ((0, 32), (4, 28))[c]

        def add(k):
            for h in range(2):
                e = m["y1"][k + h + 5, 12:28]
                for q in range(2):
                    for j in range(2):
                        at = pl.ds(8 + j, 16, stride=2)
                        i = 2 * (k + h) + q + 1
                        m["y0"][i, at, :] = m["y0"][i, at, :] + e

        sweep(lo // 2, hi // 2, 2, add)
        if c == 0:
            lv0.pass_one(2, 30, 7)
            lv0.pass_two(2, 30, 7)
        else:
            lv0.pass_one(6, 26, 5)
            lv0.pass_two(7, 25, 6)

    for c in range(2):
        if c == 0:
            lv0.second_zero(0, 32, 8)
        else:
            lv0.pass_one(4, 28, 8)
            lv0.pass_two(4, 28, 8)
        send_b(c)
        if c == 0:
            gather_two(2)
            setup_level1()
            copies_s2 = exchange_tile(EX_S2, m["s2t"], m["rs2"])
        take_b(c)
        pre_level1(c)
        gather_one(c)
        copies_g[c] = exchange_tile(EX_G + c, m["g2t"].at[c], m["rg2"].at[c])
        if c == 0:
            arrive(copies_s2)
            assemble(m["s2t"], m["rs2"], m["s2"])
            make_weights(lv2, m["s2"], 8, 16, 6)
        gather_two(c)
        arrive(copies_g[c])
        assemble(m["g2t"].at[c], m["rg2"].at[c], m["g2"])
        lv2.first_zero(0, 16, 16)
        lv2.second_zero(1, 15, 14)
        if c == 0:
            m["dg3"][...] = 6.0 + gather_done(2) * 64.0
        if c == 1:
            for copies in sent:
                for copy, (dx, dy) in zip(copies, NEIGH):
                    pl.when(exists(dx, dy))(copy.wait_send)
            for k in range(3):
                wait_bytes(m["p1"].at[k, pl.ds(0, ngy - 1)], m["ags"].at[k, 0])
                wait_bytes(m["agb"].at[k, pl.ds(0, ngx - 1)], m["ags"].at[k, 2])
        coarse(gather_done(c))
        post_level2()
        post_level1(c)
        post_level0(c)

    def store(i, n, r):
        res_ref[pl.ds(i - 8, n)] = r[:, 8:24]
        sol_ref[pl.ds(i - 8, n)] = m["y0"][pl.ds(i + 1, n), 16:32]

    lv0.residual(8, 24, 8, store)


def solution(mesh):
    ngx, ngy = mesh.shape["gx"], mesh.shape["gy"]
    items = scratch_list(ngx)
    names = tuple(name for name, _ in items)

    def per_device(point_counts, face_counts):
        shape = jax.ShapeDtypeStruct(point_counts.shape, F32)
        return pl.pallas_call(
            functools.partial(kernel, ngx, ngy, names),
            out_shape=(shape, shape),
            in_specs=[pl.BlockSpec(memory_space=pltpu.HBM)] * 2,
            out_specs=(pl.BlockSpec(memory_space=pltpu.VMEM),) * 2,
            scratch_shapes=[spec for _, spec in items],
            compiler_params=pltpu.CompilerParams(
                collective_id=0, has_side_effects=True, vmem_limit_bytes=54880 * 1024
            ),
            name="poisson",
        )(point_counts, face_counts)

    return jax.shard_map(
        per_device,
        mesh=mesh,
        in_specs=(P("gx", "gy", None), P(None, "gx", "gy", None)),
        out_specs=(P("gx", "gy", None), P("gx", "gy", None)),
        check_vma=False,
    )
```

```python
import functools

import jax
import jax.numpy as jnp
from jax import lax
from jax.experimental import pallas as pl
from jax.experimental.pallas import tpu as pltpu
from jax.sharding import PartitionSpec as P


MESH = pl.DeviceIdType.MESH
F32 = jnp.float32
BF16 = jnp.bfloat16
NEIGH = ((-1, -1), (-1, 1), (1, -1), (1, 1), (-1, 0), (1, 0), (0, -1), (0, 1))

CENTRE = 0.5 * (2.0 + 0.3)
RADIUS = 0.5 * (2.0 - 0.3)
RATIO = CENTRE / RADIUS
MOM = 1.0 / RATIO
MOM2 = 1.0 / (2.0 * RATIO - MOM)
C1 = 1.0 / CENTRE
CA = MOM2 * MOM
CB = 2.0 * MOM2 / RADIUS
K0 = 1.0 - C1
K1 = 1.0 + CA - CB
K2 = CB / C1
COARSE_ITERS = 6


def lanes(shape):
    return lax.broadcasted_iota(jnp.int32, shape, len(shape) - 1)


def rows(shape):
    return lax.broadcasted_iota(jnp.int32, shape, len(shape) - 2)


def roll(v, shift, axis):
    return pltpu.roll(v, shift, axis)


def zpair(v, width):
    axis = v.ndim - 1
    low = (lanes(v.shape) & width) == 0
    return v + jnp.where(low, roll(v, 128 - width, axis), roll(v, width, axis))


def side_sum(c, up, dn, shift):
    ax = c.ndim - 2
    count = c.shape[ax]
    lane = lanes(c.shape)
    total = up + dn
    total = total + (roll(c, 1, ax) + roll(c, count - 1, ax))
    low = jnp.where(lane < shift, 0.0, roll(c, shift, ax + 1))
    high = jnp.where(lane >= 128 - shift, 0.0, roll(c, 128 - shift, ax + 1))
    return total + (low + high)


def sweep(lo, hi, step, body):
    def one(k, carry):
        body(lo + k * step)
        return carry

    lax.fori_loop(0, (hi - lo) // step, one, 0, unroll=True)


def far_first(ngx):
    return sorted(range(1, ngx), key=lambda o: -(min(o % 8, 8 - o % 8) + min(o // 8, 4 - o // 8)))


class Level:
    def __init__(self, x, y, g, w, dg, depth):
        self.x, self.y, self.g, self.w, self.dg = x, y, g, w, dg
        self.depth = depth
        self.shift = 2**depth
        self.count = g.shape[1]
        self.mid = slice(8, 8 + self.count)

    def around(self, src, i, n):
        c = src[pl.ds(i + 1, n), self.mid]
        lane = lanes(c.shape)
        total = src[pl.ds(i + 2, n), self.mid] + src[pl.ds(i, n), self.mid]
        total = total + (src[pl.ds(i + 1, n), 7 : 7 + self.count] + src[pl.ds(i + 1, n), 9 : 9 + self.count])
        low = jnp.where(lane < self.shift, 0.0, roll(c, self.shift, 2))
        high = jnp.where(lane >= 128 - self.shift, 0.0, roll(c, 128 - self.shift, 2))
        return c, (total + self.g[pl.ds(i, n)]) + (low + high)

    def first_zero(self, lo, hi, n):
        def body(i):
            self.x[pl.ds(i + 1, n), self.mid] = self.g[pl.ds(i, n)] * self.w[pl.ds(i, n)]

        sweep(lo, hi, n, body)

    def second_zero(self, lo, hi, n):
        def body(i):
            c, t = self.around(self.x, i, n)
            self.y[pl.ds(i + 1, n), self.mid] = K1 * c + K2 * (t * self.w[pl.ds(i, n)])

        sweep(lo, hi, n, body)

    def pass_one(self, lo, hi, n):
        def body(i):
            c, t = self.around(self.y, i, n)
            self.x[pl.ds(i + 1, n), self.mid] = K0 * c + t * self.w[pl.ds(i, n)]

        sweep(lo, hi, n, body)

    def pass_two(self, lo, hi, n):
        def body(i):
            c, t = self.around(self.x, i, n)
            old = self.y[pl.ds(i + 1, n), self.mid]
            self.y[pl.ds(i + 1, n), self.mid] = (K1 * c - CA * old) + K2 * (t * self.w[pl.ds(i, n)])

        sweep(lo, hi, n, body)

    def residual(self, lo, hi, n, store):
        def body(i):
            c, t = self.around(self.y, i, n)
            store(i, n, t - self.dg[pl.ds(i, n)] * c)

        sweep(lo, hi, n, body)


def scratch_list(ngx):
    v = pltpu.VMEM
    return (
        ("fcv", v((3, 16, 16, 128), jnp.int32)),
        ("pcv", v((16, 16, 128), jnp.int32)),
        ("ext", v((32, 4, 16, 128), BF16)),
        ("exs", v((2, 16, 128), BF16)),
        ("rex", v((8, 2, 16, 128), BF16)),
        ("s1p", v((4, 16, 128), BF16)),
        ("rs1", v((8, 4, 16, 128), BF16)),
        ("scrown", v((16, 16, 128), F32)),
        ("s1own", v((8, 8, 128), F32)),
        ("fy1", v((32, 128), F32)),
        ("fy2", v((32, 128), F32)),
        ("x0", v((34, 48, 128), F32)),
        ("y0", v((34, 48, 128), F32)),
        ("g0", v((32, 32, 128), F32)),
        ("w0", v((32, 32, 128), F32)),
        ("dg0", v((32, 32, 128), F32)),
        ("r0", v((16, 16, 128), F32)),
        ("pk", v((2, 4, 8, 128), F32)),
        ("rb", v((2, 8, 4, 8, 128), F32)),
        ("x1", v((26, 40, 128), F32)),
        ("y1", v((26, 40, 128), F32)),
        ("g1", v((24, 24, 128), F32)),
        ("s1", v((24, 24, 128), F32)),
        ("w1", v((24, 24, 128), F32)),
        ("dg1", v((24, 24, 128), F32)),
        ("r1", v((16, 24, 128), F32)),
        ("s2t", v((8, 8, 128), F32)),
        ("w2t", v((8, 8, 128), F32)),
        ("rs2", v((8, 8, 8, 128), F32)),
        ("g2t", v((2, 8, 8, 128), F32)),
        ("rg2", v((2, 8, 8, 8, 128), F32)),
        ("x2", v((18, 32, 128), F32)),
        ("y2", v((18, 32, 128), F32)),
        ("g2", v((16, 16, 128), F32)),
        ("s2", v((16, 16, 128), F32)),
        ("w2", v((16, 16, 128), F32)),
        ("dg2", v((16, 16, 128), F32)),
        ("pe2", v((8, 16, 128), F32)),
        ("tile", v((3, 4, 128), F32)),
        ("p1", v((3, 7, 4, 128), F32)),
        ("agb", v((3, ngx, 4, 128), F32)),
        ("dg3", v((ngx // 2, 8, 128), F32)),
        ("e3", v((ngx // 2, 8, 128), F32)),
        ("snd", pltpu.SemaphoreType.DMA((8, 8))),
        ("rcv", pltpu.SemaphoreType.DMA((8, 8))),
        ("ags", pltpu.SemaphoreType.DMA((3, 4))),
        ("loc", pltpu.SemaphoreType.DMA((2,))),
    )


EX_IN, EX_FACE, EX_S1, EX_S2, EX_B, EX_G = 0, 1, 2, 3, 4, 6


def kernel(ngx, ngy, names, pc_hbm, fc_hbm, sol_ref, res_ref, *scratch):
    m = dict(zip(names, scratch))
    gx = lax.axis_index("gx")
    gy = lax.axis_index("gy")
    half = ngx // 2
    nx0, ny0 = 16 * ngx, 16 * ngy

    def wrap_x(v):
        return lax.rem(v + ngx, ngx)

    def wrap_y(v):
        return lax.rem(v + ngy, ngy)

    copy_p = pltpu.make_async_copy(pc_hbm, m["pcv"], m["loc"].at[0])
    copy_f = pltpu.make_async_copy(fc_hbm, m["fcv"], m["loc"].at[1])
    copy_p.start()
    copy_f.start()

    barrier = pltpu.get_barrier_semaphore()
    met = [(o, 0) for o in far_first(ngx)]
    met += [(dx, dy) for dx, dy in NEIGH if dx != 0 and dy != 0]
    met += [(0, o) for o in range(1, ngy)]
    for dx, dy in met:
        pl.semaphore_signal(
            barrier, inc=1, device_id=(wrap_x(gx + dx), wrap_y(gy + dy)), device_id_type=MESH
        )

    spans = {1: (8, 8, 0), 0: (0, 16, 8), -1: (0, 8, 24)}
    tiles = {1: (1, 1, 0), 0: (0, 2, 1), -1: (0, 1, 3)}

    def exists(dx, dy):
        x, y = gx + dx, gy + dy
        return (x >= 0) & (x < ngx) & (y >= 0) & (y < ngy)

    copy_f.wait()
    copy_p.wait()
    fcv, pcv = m["fcv"], m["pcv"]

    def own_rows(i):
        def counts(d, at, n):
            return fcv[d, pl.ds(at, n)].astype(F32) * 0.125

        f0, f1, f2 = counts(0, i, 4), counts(1, i, 4), counts(2, i, 4)
        before = jnp.where(i > 0, counts(0, jnp.maximum(i - 1, 0), 1), 0.0)
        low_x = jnp.concatenate([before, f0[:3]], axis=0)
        low_y = jnp.where(rows(f1.shape) == 0, 0.0, roll(f1, 1, 1))
        low_z = jnp.where(lanes(f2.shape) == 0, 0.0, roll(f2, 1, 2))
        src = (low_x - f0) + (low_y - f1) + (low_z - f2)
        scr = pcv[pl.ds(i, 4)].astype(F32) * 0.25
        m["scrown"][pl.ds(i, 4)] = scr
        for t in range(2):
            part = slice(8 * t, 8 * t + 8)
            m["ext"][pl.ds(i + 8, 4), t + 1] = jnp.concatenate([src[:, part], scr[:, part]], axis=1).astype(BF16)

    sweep(0, 16, 4, own_rows)

    tile_shape = (8, 128)
    sub = rows(tile_shape)
    lane = lanes(tile_shape)
    face_x = fcv[0, 15].astype(F32) * 0.125
    own_fx = [face_x[0:8], face_x[8:16]]
    own_fy = []
    for h in range(2):
        total = jnp.zeros(tile_shape, F32)
        for r in range(8):
            row = fcv[1, 8 * h + r, 15:16].astype(F32) * 0.125
            total = jnp.where(sub == r, row, total)
        own_fy.append(total)
    for t in range(2):
        m["exs"][t] = jnp.concatenate([own_fx[t], own_fy[t]], axis=0).astype(BF16)

    pl.semaphore_wait(barrier, len(met))

    sent = []

    def exchange(kind, make):
        copies = []
        for n, (dx, dy) in enumerate(NEIGH):
            src, dst = make(n, dx, dy)
            copy = pltpu.make_async_remote_copy(
                src_ref=src,
                dst_ref=dst,
                send_sem=m["snd"].at[kind, n],
                recv_sem=m["rcv"].at[kind, n],
                device_id=(wrap_x(gx + dx), wrap_y(gy + dy)),
                device_id_type=MESH,
            )
            pl.when(exists(dx, dy))(copy.start)
            copies.append(copy)
        sent.append(copies)
        return copies

    def arrive(copies):
        for copy, (dx, dy) in zip(copies, NEIGH):
            pl.when(exists(-dx, -dy))(copy.wait_recv)

    def from_source(px, py):
        return NEIGH.index((-px, -py))

    def make_in(n, dx, dy):
        xs, xn, xd = spans[dx]
        ys, yn, yd = tiles[dy]
        src = m["ext"].at[pl.ds(xs + 8, xn), pl.ds(ys + 1, yn)]
        dst = m["ext"].at[pl.ds(xd, xn), pl.ds(yd, yn)]
        return src, dst

    def make_face(n, dx, dy):
        first, count = (0, 2) if (dx, dy) in ((1, 0), (0, 1)) else ((1, 1) if (dx, dy) == (1, 1) else (0, 1))
        part = pl.ds(first, count)
        return m["exs"].at[part], m["rex"].at[n, part]

    copies_face = exchange(EX_FACE, make_face)
    copies_in = exchange(EX_IN, make_in)

    for n, (dx, dy) in enumerate(NEIGH):

        @pl.when(jnp.logical_not(exists(-dx, -dy)))
        def _():
            _, xn, xd = spans[dx]
            _, yn, yd = tiles[dy]
            m["ext"][xd : xd + xn, yd : yd + yn] = jnp.zeros((xn, yn, 16, 128), BF16)
            for name in ("rex", "rs1", "rs2"):
                m[name][n] = jnp.zeros(m[name].shape[1:], m[name].dtype)
            for name in ("rb", "rg2"):
                for c in range(2):
                    m[name][c, n] = jnp.zeros(m[name].shape[2:], F32)

    for name in ("x0", "y0", "x1", "y1", "x2", "y2"):
        ref = m[name]
        count, width = ref.shape[:2]
        ref[0] = jnp.zeros((width, 128), F32)
        ref[count - 1] = jnp.zeros((width, 128), F32)
        ref[1 : count - 1, 0:8] = jnp.zeros((count - 2, 8, 128), F32)
        ref[1 : count - 1, width - 8 : width] = jnp.zeros((count - 2, 8, 128), F32)

    own1 = []
    for i in range(8):
        total = jnp.zeros(tile_shape, F32)
        for q in range(2):
            for j in range(2):
                total = total + m["scrown"][2 * i + q, pl.ds(j, 8, stride=2), :]
        v = zpair(total, 1) * 0.125
        m["s1own"][i] = v
        own1.append(v)
    for k in range(4):
        m["s1p"][k] = jnp.concatenate([own1[2 * k], own1[2 * k + 1]], axis=0).astype(BF16)
    copies_s1 = exchange(EX_S1, lambda n, dx, dy: (m["s1p"], m["rs1"].at[n]))

    own3 = []
    for xi in range(2):
        pair = jnp.zeros((4, 128), F32)
        for q in range(2):
            quad = jnp.zeros((4, 128), F32)
            for h in range(2):
                for j in range(2):
                    quad = quad + m["s1own"][4 * xi + 2 * q + h, pl.ds(j, 4, stride=2), :]
            pair = pair + zpair(quad, 2) * 0.125
        pair = zpair(pair, 4) * 0.125
        own3 += [pair[0:1] + pair[1:2], pair[2:3] + pair[3:4]]
    m["tile"][2] = jnp.concatenate(own3, axis=0)

    def gather_one(c):
        for o in range(1, ngy):
            pltpu.make_async_remote_copy(
                src_ref=m["tile"].at[c],
                dst_ref=m["p1"].at[c, o - 1],
                send_sem=m["ags"].at[c, 0],
                recv_sem=m["ags"].at[c, 1],
                device_id=(gx, wrap_y(gy + o)),
                device_id_type=MESH,
            ).start()

    def wait_bytes(ref, sem):
        pltpu.make_async_copy(ref, ref, sem).wait()

    def gather_two(c):
        wait_bytes(m["p1"].at[c, pl.ds(0, ngy - 1)], m["ags"].at[c, 1])
        slot = lanes((4, 128)) & 7
        total = jnp.where(slot == gy, m["tile"][c], 0.0)
        for o in range(1, ngy):
            total = jnp.where(slot == wrap_y(gy - o), m["p1"][c, o - 1], total)
        m["agb"][c, gx] = total

        for o in far_first(ngx):
            pltpu.make_async_remote_copy(
                src_ref=m["agb"].at[c, gx],
                dst_ref=m["agb"].at[c, gx],
                send_sem=m["ags"].at[c, 2],
                recv_sem=m["ags"].at[c, 3],
                device_id=(wrap_x(gx + o), gy),
                device_id_type=MESH,
            ).start()

    def gather_done(c):
        wait_bytes(m["agb"].at[c, pl.ds(0, ngx - 1)], m["ags"].at[c, 3])
        return jnp.concatenate([m["agb"][c, 0:half], m["agb"][c, half:ngx]], axis=1)

    gather_one(2)

    arrive(copies_face)
    gate_x = jnp.where(gx > 0, 1.0, 0.0)
    gate_y = jnp.where(gy > 0, 1.0, 0.0)

    def face(px, py, t):
        return m["rex"][from_source(px, py), t].astype(F32)

    m["fy1"][0:8] = face(-1, -1, 1)[8:16] * gate_y
    m["fy1"][8:16] = face(0, -1, 0)[8:16] * gate_y
    m["fy1"][16:24] = face(0, -1, 1)[8:16] * gate_y
    m["fy1"][24:32] = face(1, -1, 0)[8:16] * gate_y
    m["fy2"][0:8] = face(-1, 0, 1)[8:16]
    m["fy2"][8:16] = own_fy[0]
    m["fy2"][16:24] = own_fy[1]
    m["fy2"][24:32] = face(1, 0, 0)[8:16]
    arrive(copies_in)

    def inside(shape, i, level, off):
        x = lax.broadcasted_iota(jnp.int32, shape, 0) + (i - off + gx * (16 >> level))
        y = rows(shape) + (gy * (16 >> level) - off)
        return (x >= 0) & (x < (nx0 >> level)) & (y >= 0) & (y < (ny0 >> level))

    def weight(dg, i, level, off):
        return jnp.where(inside(dg.shape, i, level, off), C1 / dg, 0.0)

    def unpack_in(n, i):
        for t in range(4):
            part = slice(8 * t, 8 * t + 8)
            pair = m["ext"][pl.ds(i, n), t].astype(F32)
            src = pair[:, 0:8]
            if t % 2 == 1:
                edge = m["fy1" if t == 1 else "fy2"]
                src = jnp.concatenate(
                    [(src[q] + jnp.where(sub == 0, edge[pl.ds(i + q, 1)], 0.0))[None] for q in range(n)], axis=0
                )
            dg = 6.0 + pair[:, 8:16]
            x = lax.broadcasted_iota(jnp.int32, dg.shape, 0) + (i - 8 + gx * 16)
            y = rows(dg.shape) + (gy * 16 - 8 + 8 * t)
            mask = (x >= 0) & (x < nx0) & (y >= 0) & (y < ny0)
            w = jnp.where(mask, C1 / dg, 0.0)
            m["g0"][pl.ds(i, n), part] = src
            m["dg0"][pl.ds(i, n), part] = dg
            m["w0"][pl.ds(i, n), part] = w
            m["x0"][pl.ds(i + 1, n), 8 * t + 8 : 8 * t + 16] = src * w

    sweep(6, 26, 4, functools.partial(unpack_in, 4))
    for t, (py, k) in enumerate(((-1, 1), (0, 0), (0, 1), (1, 0))):
        part = slice(8 * t, 8 * t + 8)
        upper = own_fx[k] if py == 0 else face(0, py, k)[0:8]
        for at, extra in ((8, face(-1, py, k)[0:8] * gate_x), (24, upper)):
            total = m["g0"][at, part] + extra
            m["g0"][at, part] = total
            m["x0"][at + 1, 8 * t + 8 : 8 * t + 16] = total * m["w0"][at, part]

    lv0 = Level(m["x0"], m["y0"], m["g0"], m["w0"], m["dg0"], 0)
    lv1 = Level(m["x1"], m["y1"], m["g1"], m["w1"], m["dg1"], 1)
    lv2 = Level(m["x2"], m["y2"], m["g2"], m["w2"], m["dg2"], 2)

    def make_weights(level, scr, step, count, off):
        def body(i):
            dg = 6.0 + scr[pl.ds(i, step)] * float(4**level.depth)
            level.dg[pl.ds(i, step)] = dg
            level.w[pl.ds(i, step)] = weight(dg, i, level.depth, off)

        sweep(0, count, step, body)

    odd = (lane & 1) == 1
    copies_b = [None, None]
    copies_g = [None, None]

    def send_b(c):
        def store(i, n, r):
            m["r0"][pl.ds(i - 8, n)] = r[:, 8:24]

        lv0.residual(8, 24, 8, store)
        fine = []
        for i in range(8):
            total = jnp.zeros(tile_shape, F32)
            for q in range(2):
                for j in range(2):
                    total = total + m["r0"][2 * i + q, pl.ds(j, 8, stride=2), :]
            v = zpair(total, 1) * 0.5
            m["g1"][8 + i, 8:16] = v
            fine.append(v)
        for k in range(4):
            m["pk"][c, k] = jnp.where(odd, fine[2 * k + 1], fine[2 * k])

        def make(n, dx, dy):
            count = 4 if dx == 0 or (c == 0 and dy == 0) else 3
            part = pl.ds(4 - count if dx == 1 else 0, count)
            return m["pk"].at[c, part], m["rb"].at[c, n, part]

        copies_b[c] = exchange(EX_B + c, make)

    def take_b(c):
        arrive(copies_b[c])
        for n, (dx, dy) in enumerate(NEIGH):
            base = 8 - 8 * dx
            part = slice(8 - 8 * dy, 16 - 8 * dy)
            ks = range(4) if dx == 0 or (c == 0 and dy == 0) else (range(1, 4) if dx == 1 else range(3))
            for k in ks:
                v = m["rb"][c, n, k]
                m["g1"][base + 2 * k, part] = jnp.where(odd, roll(v, 1, 1), v)
                m["g1"][base + 2 * k + 1, part] = jnp.where(odd, v, roll(v, 127, 1))

    def setup_level1():
        arrive(copies_s1)
        for i in range(8):
            m["s1"][8 + i, 8:16] = m["s1own"][i]
        for n, (dx, dy) in enumerate(NEIGH):
            base = 8 - 8 * dx
            part = slice(8 - 8 * dy, 16 - 8 * dy)
            for k in range(4):
                v = m["rs1"][n, k].astype(F32)
                m["s1"][base + 2 * k, part] = v[0:8]
                m["s1"][base + 2 * k + 1, part] = v[8:16]
        make_weights(lv1, m["s1"], 8, 24, 8)
        for i in range(8):
            total = jnp.zeros(tile_shape, F32)
            for q in range(2):
                for j in range(2):
                    total = total + m["s1"][4 + 2 * i + q, pl.ds(4 + j, 8, stride=2), :]
            m["s2t"][i] = zpair(total, 2) * 0.125
        m["w2t"][...] = weight(6.0 + m["s2t"][...] * 16.0, 0, 2, 2)

    def exchange_tile(kind, src, dst):
        def make(n, dx, dy):
            part = {1: pl.ds(0, 4), 0: pl.ds(0, 8), -1: pl.ds(4, 4)}[dx]
            return src.at[part], dst.at[n, part]

        return exchange(kind, make)

    def assemble(own, got, out):
        for i in range(16):
            px = -1 if i < 4 else (0 if i < 12 else 1)
            r = i - 4 * px - 4
            for py, part in ((-1, slice(0, 8)), (1, slice(8, 16)), (0, slice(4, 12))):
                out[i, part] = own[r] if (px, py) == (0, 0) else got[from_source(px, py), r]

    def pre_level1(c):
        lv1.first_zero(2, 22, 10)
        lv1.second_zero(3, 21, 9)

        def store(i, n, r):
            m["r1"][pl.ds(i - 4, n)] = r

        lv1.residual(4, 20, 8, store)
        small = []
        for i in range(8):
            total = jnp.zeros(tile_shape, F32)
            for q in range(2):
                for j in range(2):
                    total = total + m["r1"][2 * i + q, pl.ds(4 + j, 8, stride=2), :]
            small.append((zpair(total, 2) * 0.5)[None])
        g = jnp.concatenate(small, axis=0)
        m["g2t"][c] = g
        dg = 6.0 + m["s2t"][...] * 16.0
        w = m["w2t"][...]
        zero = jnp.zeros((1, 8, 128), F32)

        def around(v):
            up = jnp.concatenate([v[1:], zero], axis=0)
            dn = jnp.concatenate([zero, v[:-1]], axis=0)
            return g + side_sum(v, up, dn, 4)

        v = g * w
        v = K1 * v + K2 * (around(v) * w)
        r = around(v) - dg * v
        parts = []
        for xi in range(2):
            t = r[2 + 2 * xi] + r[3 + 2 * xi]
            t = zpair(t + roll(t, 7, 0), 4) * 0.5
            parts += [t[2:3], t[4:5]]
        m["tile"][c] = jnp.concatenate(parts, axis=0)

    def dot(a, b):
        t = a * b
        while t.shape[0] > 1:
            h = t.shape[0] // 2
            t = t[:h] + t[h:]
        t = jnp.sum(t[0], axis=0, keepdims=True)
        return jnp.sum(t, axis=1, keepdims=True)[None]

    full = (half, 8, 128)
    lane3 = lanes(full)
    sub3 = rows(full)
    slot3 = lane3 & 7
    even_y = (sub3 & 1) == 0
    even_x = (sub3 & 2) == 0
    low_y = even_y & (slot3 > 0)
    high_y = jnp.logical_not(even_y) & (slot3 < ngy - 1)

    def image3(f, dg):
        swap = jnp.where(even_y, roll(f, 7, 1), roll(f, 1, 1))
        total = swap + jnp.where(low_y, roll(swap, 1, 2), jnp.where(high_y, roll(swap, 127, 2), 0.0))
        left = roll(f, 6, 1)
        right = roll(f, 2, 1)
        after = jnp.where(sub < 4, left[0], 0.0)[None]
        ahead = jnp.where(sub >= 4, right[half - 1], 0.0)[None]
        nxt = jnp.concatenate([right[1:], after], axis=0)
        prv = jnp.concatenate([ahead, left[:-1]], axis=0)
        total = total + jnp.where(even_x, left + prv, right + nxt)
        total = total + jnp.where(lane3 < 8, 0.0, roll(f, 8, 2))
        total = total + jnp.where(lane3 >= 120, 0.0, roll(f, 120, 2))
        q = dg * f - total
        return q if ngy == 8 else jnp.where(slot3 < ngy, q, 0.0)

    def coarse(r):
        dg = m["dg3"][...]
        x = p = q = rr_old = curve = None
        for it in range(COARSE_ITERS):
            image = image3(r, dg)
            rr = dot(r, r)
            rar = dot(r, image)
            if it == 0:
                p, q, curve = r, image, rar
            else:
                beta = rr / rr_old
                curve = rar - beta * beta * curve
                p = r + beta * p
                q = image + beta * q
            alpha = rr / curve
            x = alpha * p if it == 0 else x + alpha * p
            if it + 1 < COARSE_ITERS:
                r = r - alpha * q
            rr_old = rr
        m["e3"][...] = x

    pick = (lane - (lane & 7)) + jnp.clip(gy - 2 + ((sub + 1) >> 1), 0, ngy - 1)

    def post_level2():
        for k in range(8):
            a, xi = (k - 3) >> 1, (k - 3) & 1
            at = wrap_x(gx + a)
            b = at // half
            v = at - b * half
            low = m["e3"][v, pl.ds(4 * b + 2 * xi, 1)]
            high = m["e3"][v, pl.ds(4 * b + 2 * xi + 1, 1)]
            t = jnp.where((sub & 1) == 1, low, high)
            t = jnp.take_along_axis(t, pick, axis=1, mode="promise_in_bounds")
            m["pe2"][k, pl.ds(0, 8, stride=2), :] = t
            m["pe2"][k, pl.ds(1, 8, stride=2), :] = t
        for i in range(16):
            m["y2"][i + 1, 8:24] = m["y2"][i + 1, 8:24] + jnp.where(m["w2"][i] != 0.0, m["pe2"][i // 2], 0.0)
        lv2.pass_one(1, 15, 14)
        lv2.pass_two(2, 14, 12)

    def post_level1(c):
        lo, hi = ((2, 22), (4, 20))[c]
        for i in range(lo, hi):
            e = m["y2"][i // 2 + 3, 10:22]
            for j in range(2):
                at = pl.ds(8 + j, 12, stride=2)
                m["y1"][i + 1, at, :] = m["y1"][i + 1, at, :] + e
        if c == 0:
            lv1.pass_one(3, 21, 9)
            lv1.pass_two(4, 20, 8)
        else:
            lv1.pass_one(5, 19, 7)
            lv1.pass_two(6, 18, 6)

    def post_level0(c):
        lo, hi = ((0, 32), (4, 28))[c]

        def add(k):
            for h in range(2):
                e = m["y1"][k + h + 5, 12:28]
                for q in range(2):
                    for j in range(2):
                        at = pl.ds(8 + j, 16, stride=2)
                        i = 2 * (k + h) + q + 1
                        m["y0"][i, at, :] = m["y0"][i, at, :] + e

        sweep(lo // 2, hi // 2, 2, add)
        if c == 0:
            lv0.pass_one(2, 30, 7)
            lv0.pass_two(2, 30, 7)
        else:
            lv0.pass_one(6, 26, 5)
            lv0.pass_two(7, 25, 6)

    for c in range(2):
        if c == 0:
            lv0.second_zero(7, 25, 6)
        else:
            lv0.pass_one(6, 26, 5)
            lv0.pass_two(7, 25, 6)
        send_b(c)
        if c == 0:
            gather_two(2)
            setup_level1()
            copies_s2 = exchange_tile(EX_S2, m["s2t"], m["rs2"])
            for lo in (0, 26):
                sweep(lo, lo + 6, 2, functools.partial(unpack_in, 2))
            lv0.second_zero(1, 7, 6)
            lv0.second_zero(25, 31, 6)
        else:
            for lo in (4, 26):
                lv0.pass_one(lo, lo + 2, 2)
            for lo in (5, 25):
                lv0.pass_two(lo, lo + 2, 2)
        take_b(c)
        pre_level1(c)
        gather_one(c)
        copies_g[c] = exchange_tile(EX_G + c, m["g2t"].at[c], m["rg2"].at[c])
        if c == 0:
            arrive(copies_s2)
            assemble(m["s2t"], m["rs2"], m["s2"])
            make_weights(lv2, m["s2"], 8, 16, 6)
        gather_two(c)
        if c == 0:
            for at in (1, 22):
                lv1.first_zero(at, at + 1, 1)
            for at in (2, 21):
                lv1.second_zero(at, at + 1, 1)
        arrive(copies_g[c])
        assemble(m["g2t"].at[c], m["rg2"].at[c], m["g2"])
        lv2.first_zero(0, 16, 16)
        lv2.second_zero(1, 15, 14)
        if c == 0:
            m["dg3"][...] = 6.0 + gather_done(2) * 64.0
        if c == 1:
            for copies in sent:
                for copy, (dx, dy) in zip(copies, NEIGH):
                    pl.when(exists(dx, dy))(copy.wait_send)
            for k in range(3):
                wait_bytes(m["p1"].at[k, pl.ds(0, ngy - 1)], m["ags"].at[k, 0])
                wait_bytes(m["agb"].at[k, pl.ds(0, ngx - 1)], m["ags"].at[k, 2])
        coarse(gather_done(c))
        post_level2()
        post_level1(c)
        post_level0(c)

    def store(i, n, r):
        res_ref[pl.ds(i - 8, n)] = r[:, 8:24]
        sol_ref[pl.ds(i - 8, n)] = m["y0"][pl.ds(i + 1, n), 16:32]

    lv0.residual(8, 24, 8, store)


def solution(mesh):
    ngx, ngy = mesh.shape["gx"], mesh.shape["gy"]
    items = scratch_list(ngx)
    names = tuple(name for name, _ in items)

    def per_device(point_counts, face_counts):
        shape = jax.ShapeDtypeStruct(point_counts.shape, F32)
        return pl.pallas_call(
            functools.partial(kernel, ngx, ngy, names),
            out_shape=(shape, shape),
            in_specs=[pl.BlockSpec(memory_space=pltpu.HBM)] * 2,
            out_specs=(pl.BlockSpec(memory_space=pltpu.VMEM),) * 2,
            scratch_shapes=[spec for _, spec in items],
            compiler_params=pltpu.CompilerParams(
                collective_id=0, has_side_effects=True, vmem_limit_bytes=54880 * 1024
            ),
            name="poisson",
        )(point_counts, face_counts)

    return jax.shard_map(
        per_device,
        mesh=mesh,
        in_specs=(P("gx", "gy", None), P(None, "gx", "gy", None)),
        out_specs=(P("gx", "gy", None), P("gx", "gy", None)),
        check_vma=False,
    )
```
